32 devices in a mesh: region: 1, drive: 16 (over z, y, core), street: 2 (over x).
Axes of the slice: x: 2, y: 2, z: 4, core: 2. Of those that a mesh axis runs over, the one named last changes fastest.
Arguments:
- pt_count: int32 [64], P(('region', 'drive')), may hold values from 16 to 256, as said below
- partner_dev: int32 [64, 4], P('region'), may hold values from 0 to 15, all different within a row; in each aligned block of 4 rows (0 to 3, 4 to 7, ...) at most 2 rows name the same one
- partner_pick: int32 [64, 4], P('region'), may hold values from 0 to 3
- knot_own: int32 [64, 256], P(('region', 'drive'), 'street'), may hold values from 0 to 508
- knot_partner: int32 [64, 256], P(('region', 'drive'), 'street'), may hold values from 0 to 508
- match_slot: int32 [64, 256], P(('region', 'drive'), 'street'), may hold values from 0 to 3
- spline: float32 [2, 64, 256], P(None, ('region', 'drive'), 'street'), may hold values from 0 to 1
- geometry: float32 [12, 64, 256], P(None, ('region', 'drive'), 'street'), may hold values from -6 to 6
- point_weight: float32 [64, 256], P(('region', 'drive'), 'street'), may hold values from 0.2 to 5
- point_resid: float32 [64, 256], P(('region', 'drive'), 'street'), may hold values from -6 to 6
Outputs:
- step: float32 [64, 8, 384], P(('region', 'drive'), 'street')
- cg_resid: float32 [64, 8, 384], P(('region', 'drive'), 'street')
The draws below stay inside these ranges and needn't reach their ends.
Inputs may be any that keep to these rules, and one draw needn't show every extreme that they name: `pt_count`: some drive has exactly 256 live slots; slots at or beyond a drive's count are ignored. `partner_dev`: the 4 partners of a drive lie on different indices of drive. Among the drives of one index of drive (aligned blocks of 4 rows) at most 2 name any one index, a bound that some block reaches.
All inputs are finite; a program needn't handle non-finite values.
Results may differ from the reference program's by a relative error of at most 0.00011.
Values sent between devices are 32-bit elements; how exact they have to be, the bound alone decides.
No kernel may reach another device: no remote copies, remote signals or barrier semaphores. Data moves between devices by JAX's collectives and lax.ppermute only.
A program may use at most 64 MiB of HBM per device.

```python
import math
import jax
import jax.numpy as jnp
import numpy as np
from jax import lax

DRV_DEV = 4
NBLK = 8
BLOCK_POINTS = 64
DOF = 6
PARAMS = 384
MATCH = 4
ITERS = 2
NDRV = 64
NPT = 256
CAP = 2
N_DRIVE = 16


def draw_pt_count(key, part):
    light_key = jax.random.fold_in(key, 11)
    heavy_key = jax.random.fold_in(key, 12)
    place_key = jax.random.fold_in(key, 13)
    light_counts = jax.random.randint(light_key, (NDRV,), NPT // 16, NPT // 4 + 1)
    heavy_flags = jax.random.randint(heavy_key, (NDRV,), 0, 8) == 0
    counts = jnp.where(heavy_flags, NPT, light_counts)
    chosen = jax.random.randint(place_key, (), 0, NDRV)
    return counts.at[chosen].set(NPT).astype(jnp.int32)


def place_ends(drawn, stream_key, smallest, largest):
    shape = drawn.shape
    index_at = [jax.random.randint(jax.random.fold_in(stream_key, axis), (), 0, shape[axis]) for axis in range(len(shape))]
    drawn = drawn.at[tuple(index_at)].set(smallest)
    longest = shape.index(max(shape))
    index_at[longest] = (index_at[longest] + 1) % shape[longest]
    return drawn.at[tuple(index_at)].set(largest)


def steps_of(stream_key, dims, pieces, low, high):
    level = 1.0
    for axis_at, parts in pieces:
        draws = jax.random.uniform(jax.random.fold_in(jax.random.fold_in(stream_key, 6), axis_at), (parts,), jnp.float32, low / len(pieces), high / len(pieces))
        level = level * jnp.repeat(jnp.exp(draws), dims[axis_at] // parts).reshape((-1,) + (1,) * (len(dims) - 1 - axis_at))
    return level


def assign_block(own_key, own, number, rows, count, top, limit, skew):
    sequence = jax.random.permutation(own_key, count)
    heavy_load, usual = load_shares(count, rows * top, limit, skew, True), load_shares(count, rows * top, limit, skew, False)
    places = jnp.arange(count)

    def named(tallies, rotation):
        used = int((tallies > 0).sum())
        fixed = max(1, used // 4)
        shifted = fixed + (places - fixed + rotation * (used - fixed)) % max(1, count - fixed)
        return jnp.zeros((count,), jnp.int32).at[sequence[jnp.where(places < fixed, places, shifted)]].set(jnp.asarray(tallies, jnp.int32))

    tallies = jnp.where(number % 4 == 0, named(heavy_load, number // 4), named(usual, number - number // 4 - 1))
    mixed = jax.random.permutation(jax.random.fold_in(own, 3), count)
    giver, sink = mixed[0:count // 2 * 2:2], mixed[1:count // 2 * 2:2]
    slack = jnp.minimum(tallies[giver] - 1, limit - tallies[sink]) // 2
    slack = jnp.where((giver == sequence[0]) | (sink == sequence[0]) | (tallies[sink] == 0), 0, jnp.maximum(slack, 0))
    shifted = jax.random.randint(jax.random.fold_in(own, 4), (count // 2,), 0, 1 << 20) % (slack + 1)
    tallies = tallies.at[giver].add(-shifted).at[sink].add(shifted)
    labels = jnp.searchsorted(jnp.cumsum(tallies), jnp.arange(rows * top), side="right").astype(jnp.int32)
    table = labels.reshape(top, rows).T
    table = table[jax.random.permutation(jax.random.fold_in(own, 1), rows)]
    rotation = jax.random.randint(jax.random.fold_in(own, 2), (rows, 1), 0, top)
    return jnp.take_along_axis(table, (jnp.arange(top)[None, :] + rotation) % top, axis=1)


def load_shares(count, total, most, slope, full):
    loads = [(1 << 20) // math.isqrt(grade ** slope) + 1 for grade in range(1, count + 1)]
    largest = most if full else min(most, max(-(-total // count), total * loads[0] // sum(loads)))
    least = 1 if total - largest >= count - 1 else 0
    given, rest = [largest] + [least] * (count - 1), total - largest - least * (count - 1)
    while rest > 0:
        movable = [i for i in range(1, count) if given[i] < largest] or [i for i in range(1, count) if given[i] < most]
        whole, remaining = sum([loads[i] for i in movable]), rest
        for i in movable:
            more = min(most - given[i], max(1, remaining * loads[i] // whole), rest)
            given[i] = given[i] + more
            rest = rest - more
    return np.array(given)


def bell_draw(key, extent, scale, bound, pieces=(), kind=jnp.bfloat16):
    result = jax.random.normal(key, extent, jnp.float32) * scale
    if len(pieces) > 0:
        result = steps_of(key, extent, pieces, -0.22, 0.18) * result
    return jnp.clip(result, min=-bound, max=bound).astype(kind)


def setup_inputs(seed: int = 0, part: int = 0) -> dict:
    streams_of = jax.random.split(jax.random.key(seed), 11)
    own_keys = jax.random.split(jax.random.fold_in(streams_of[10], part), 11)
    pt_count = draw_pt_count(jax.random.fold_in(jax.random.fold_in(streams_of[10], part), 71), part)
    partner_dev_keys = jax.random.split(jax.random.fold_in(own_keys[1], 1), NDRV // DRV_DEV)
    partner_dev_turns = jax.random.permutation(jax.random.fold_in(own_keys[1], 3), NDRV // DRV_DEV)
    partner_dev = jax.vmap(lambda own, number: assign_block(jax.random.fold_in(own_keys[1], 2), own, number, DRV_DEV, N_DRIVE, MATCH, CAP, 2))(partner_dev_keys, partner_dev_turns).reshape((NDRV, MATCH))
    partner_pick = place_ends(jax.random.randint(own_keys[2], (NDRV, MATCH), 0, DRV_DEV), jax.random.fold_in(own_keys[2], 1), 0, DRV_DEV - 1).astype(jnp.int32)
    knot_own = place_ends(jax.random.randint(own_keys[3], (NDRV, NPT), 0, NBLK * BLOCK_POINTS - 3), jax.random.fold_in(own_keys[3], 1), 0, (NBLK * BLOCK_POINTS - 3) - 1).astype(jnp.int32)
    knot_partner = place_ends(jax.random.randint(own_keys[4], (NDRV, NPT), 0, NBLK * BLOCK_POINTS - 3), jax.random.fold_in(own_keys[4], 1), 0, (NBLK * BLOCK_POINTS - 3) - 1).astype(jnp.int32)
    match_slot = place_ends(jax.random.randint(own_keys[5], (NDRV, NPT), 0, MATCH), jax.random.fold_in(own_keys[5], 1), 0, MATCH - 1).astype(jnp.int32)
    spline = jnp.clip(1.0 * jax.random.uniform(own_keys[6], (2, NDRV, NPT), jnp.float32) ** steps_of(own_keys[6], (2, NDRV, NPT), ((1, 16), (2, 2)), -0.2, 0.2), 0.0, 1.0)
    geometry = bell_draw(own_keys[7], (12, NDRV, NPT), 1.0, 6.0, ((1, 16), (2, 2)), jnp.float32)
    point_weight = jnp.clip(jnp.exp(math.log(5.0) - 3.218876 * jax.random.uniform(own_keys[8], (NDRV, NPT), jnp.float32) ** steps_of(own_keys[8], (NDRV, NPT), ((0, 16), (1, 2)), -0.2, 0.2)), 0.2, 5.0)
    point_resid = bell_draw(own_keys[9], (NDRV, NPT), 1.0, 6.0, ((0, 16), (1, 2)), jnp.float32)
    return {"pt_count": pt_count, "partner_dev": partner_dev, "partner_pick": partner_pick, "knot_own": knot_own, "knot_partner": knot_partner, "match_slot": match_slot, "spline": spline, "geometry": geometry, "point_weight": point_weight, "point_resid": point_resid}


DAMPING = 1.0


def spline_basis(position):
    remain = 1.0 - position
    cube = position * position * position
    square = position * position
    return jnp.stack([remain * remain * remain, 3.0 * cube - 6.0 * square + 4.0, -3.0 * cube + 3.0 * square + 3.0 * position + 1.0, cube]) / 6.0


def point_coeffs(position, normals):
    basis = spline_basis(position)
    return (basis[:, None] * normals[None]).reshape((4 * DOF,) + normals.shape[1:])


def spread_terms(own_values, partner_values, own_index, partner_index, own_width, partner_width):
    own_terms = jax.ops.segment_sum(own_values.reshape(-1), own_index.reshape(-1), num_segments=own_width)
    partner_terms = jax.ops.segment_sum(partner_values.reshape(-1), partner_index.reshape(-1), num_segments=partner_width)
    return own_terms, partner_terms


def reference(pt_count, partner_dev, partner_pick, knot_own, knot_partner, match_slot, spline, geometry, point_weight, point_resid):
    param_width = NBLK * PARAMS
    partner_ids = (partner_dev * DRV_DEV + partner_pick).astype(jnp.int32)
    live = jnp.arange(NPT, dtype=jnp.int32)[None, :] < pt_count[:, None]
    weights = jnp.where(live, point_weight, jnp.zeros_like(point_weight))
    offsets = jnp.arange(4 * DOF, dtype=jnp.int32)[:, None]
    entries = (knot_own, knot_partner, match_slot, jnp.moveaxis(spline, 1, 0), jnp.moveaxis(geometry, 1, 0), weights, point_resid, partner_ids, jnp.arange(NDRV, dtype=jnp.int32))

    def prepare(entry):
        own_index = entry[0][None, :] * DOF + offsets
        partner_index = entry[2][None, :] * param_width + entry[1][None, :] * DOF + offsets
        coef_own = point_coeffs(entry[3][0], entry[4][:DOF])
        coef_partner = point_coeffs(entry[3][1], entry[4][DOF:])
        return own_index, partner_index, coef_own, coef_partner

    def first_terms(entry):
        own_index, partner_index, coef_own, coef_partner = prepare(entry)
        weighted = entry[5] * entry[6]
        grad_own, grad_partner = spread_terms(-coef_own * weighted, coef_partner * weighted, own_index, partner_index, param_width, MATCH * param_width)
        diag_own, diag_partner = spread_terms(coef_own * coef_own * entry[5], coef_partner * coef_partner * entry[5], own_index, partner_index, param_width, MATCH * param_width)
        return grad_own, grad_partner, diag_own, diag_partner

    def gather_back(own_terms, partner_terms):
        return own_terms + jax.ops.segment_sum(partner_terms.reshape(NDRV * MATCH, param_width), partner_ids.reshape(-1), num_segments=NDRV)

    grad_own, grad_partner, diag_own, diag_partner = lax.map(first_terms, entries)
    gradient = gather_back(grad_own, grad_partner)
    diagonal = DAMPING + gather_back(diag_own, diag_partner)

    def hessian_apply(vector):
        def product_terms(entry):
            own_index, partner_index, coef_own, coef_partner = prepare(entry)
            own_values = vector[entry[8]]
            partner_values = vector[entry[7]].reshape(-1)
            projected = jnp.sum(coef_own * own_values[own_index], axis=0) - jnp.sum(coef_partner * partner_values[partner_index], axis=0)
            scaled = entry[5] * projected
            return spread_terms(coef_own * scaled, -coef_partner * scaled, own_index, partner_index, param_width, MATCH * param_width)

        own_terms, partner_terms = lax.map(product_terms, entries)
        return DAMPING * vector + gather_back(own_terms, partner_terms)

    solution = jnp.zeros_like(gradient)
    residual = gradient
    precond = residual / diagonal
    direction = precond
    inner_now = jnp.sum(residual * precond)
    for iteration in range(ITERS):
        image = hessian_apply(direction)
        step_size = inner_now / jnp.sum(direction * image)
        solution = solution + step_size * direction
        residual = residual - step_size * image
        precond = residual / diagonal
        inner_next = jnp.sum(residual * precond)
        direction = precond + (inner_next / inner_now) * direction
        inner_now = inner_next
    return solution.reshape(NDRV, NBLK, PARAMS), residual.reshape(NDRV, NBLK, PARAMS)
```

```python
import jax
import jax.numpy as jnp
from jax import lax
from jax.experimental import pallas as pl
from jax.experimental.pallas import tpu as pltpu
from jax.sharding import PartitionSpec as P

NBLK = 8
DOF = 6
PARAMS = 384
MATCH = 4
LANES = 128
HIGH = 4
CAP = 2
SUB = 8
F32 = jnp.float32
BF16 = jnp.bfloat16


def iota(shape, dim):
    return lax.broadcasted_iota(jnp.int32, shape, dim)


def take_lanes(values, index):
    return jnp.take_along_axis(values, index, axis=1, mode="promise_in_bounds")


def row_of(block, row, count=SUB):
    return jnp.broadcast_to(block[row : row + 1, :], (count, LANES))


def basis_of(s):
    remain = 1.0 - s
    square = s * s
    cube = square * s
    return (
        remain * remain * remain * (1.0 / 6.0),
        (3.0 * cube - 6.0 * square + 4.0) * (1.0 / 6.0),
        (-3.0 * cube + 3.0 * square + 3.0 * s + 1.0) * (1.0 / 6.0),
        cube * (1.0 / 6.0),
    )


def split_two(values):
    high = values.astype(BF16)
    low = (values - high.astype(F32)).astype(BF16)
    return jnp.concatenate([high, low], axis=1)


def spread(knot, kinds):
    low = jnp.bitwise_and(knot, LANES - 1)
    high = jnp.right_shift(knot, 7)
    hot = jnp.where(iota((LANES, LANES), 0) == jnp.broadcast_to(low[0:1], (LANES, LANES)), 1.0, 0.0)
    hot = hot.astype(BF16)
    hot = jnp.concatenate([hot, hot], axis=1)
    high32 = jnp.broadcast_to(high[0:1], (4 * SUB, LANES))
    masks = []
    for h in range(HIGH):
        mask = jnp.where(high32 == h, 1.0, 0.0).astype(BF16)
        masks.append(jnp.concatenate([mask, mask], axis=1))
    rows = []
    for kind in kinds:
        parts = split_two(jnp.concatenate(kind, axis=0))
        for h in range(HIGH):
            rows.append(parts * masks[h])
    left = jnp.concatenate(rows, axis=0)
    return lax.dot_general(left, hot, (((1,), (1,)), ((), ())), preferred_element_type=F32)


def fold_shifts(acc, base):
    lane = iota((SUB, LANES), 1)
    out = []
    before = None
    for h in range(HIGH):
        tiles = [acc[base + h * 32 + k * SUB : base + h * 32 + (k + 1) * SUB, :] for k in range(4)]
        rolled = [None] + [pltpu.roll(tiles[k], k, axis=1) for k in range(1, 4)]
        total = tiles[0]
        for k in range(1, 4):
            other = before[k] if before is not None else jnp.zeros((SUB, LANES), F32)
            total = total + jnp.where(lane >= k, rolled[k], other)
        out.append(total)
        before = rolled
    return out


def gather_value(tiles, knot, basis, normals):
    total = None
    for k in range(4):
        index = knot + k
        low = jnp.bitwise_and(index, LANES - 1)
        high = jnp.right_shift(index, 7)
        value = take_lanes(tiles[HIGH - 1], low)
        for h in range(HIGH - 1):
            value = jnp.where(high == h, take_lanes(tiles[h], low), value)
        term = basis[k] * value
        total = term if total is None else total + term
    return jnp.sum(normals * total, axis=0, keepdims=True)


def own_tile(own_ref, h, a):
    normals = own_ref[h, a, 0:SUB, :]
    info = own_ref[h, a, SUB : 2 * SUB, :]
    return normals, row_of(info, 0).astype(jnp.int32), basis_of(row_of(info, 1)), row_of(info, 2)


def inc_tile(inc_ref, block, rank):
    normals = inc_ref[block, pl.ds(pl.multiple_of(rank * SUB, SUB), SUB), :]
    info = inc_ref[block, 2 * SUB : 3 * SUB, :]
    info = jnp.where(rank == 0, info, jnp.concatenate([info[4:8], info[0:4]], axis=0))
    return normals, row_of(info, 0).astype(jnp.int32), basis_of(row_of(info, 1)), row_of(info, 2)


def decode(code, street_size):
    pick = jnp.bitwise_and(code, 3)
    tile = jnp.right_shift(code, 2)
    rank = jnp.bitwise_and(tile, 1)
    block = jnp.right_shift(tile, 1)
    lane = lax.div(block, street_size)
    part = block - lane * street_size
    return pick, rank, block, lane, part


def send_kernel(
    meta, counts, dev, picks, knot_own, knot_par, match, spline, geometry, weight, resid,
    send, own, tab, filled, taken, normals_s, info_s, match_s,
):
    drives = counts.shape[0]
    lanes = send.shape[0]
    street_size = send.shape[1]
    lane = meta[0]
    street = meta[1]
    for j in range(lanes):
        taken[j] = 0
        filled[2 * j] = -1
        filled[2 * j + 1] = -1
    for a in range(drives):
        for m in range(MATCH):
            e = a * MATCH + m
            dest = dev[lane * drives + a, m]
            rank = taken[dest]
            taken[dest] = rank + 1
            tab[e] = dest
            tab[drives * MATCH + e] = rank
            filled[2 * dest + rank] = e
    slot = street * LANES + iota((1, LANES), 1)
    zero1 = jnp.zeros((1, LANES), F32)
    for a in range(drives):
        w = jnp.where(slot < counts[a], weight[a : a + 1, :], 0.0)
        root = jnp.sqrt(w)
        rho = -(root * resid[a : a + 1, :])
        own[a, 0:SUB, :] = jnp.concatenate(
            [geometry[d, a : a + 1, :] * root for d in range(DOF)] + [zero1] * 2, axis=0
        )
        own[a, SUB : 2 * SUB, :] = jnp.concatenate(
            [knot_own[a : a + 1, :].astype(F32), spline[0, a : a + 1, :], rho] + [zero1] * 5, axis=0
        )
        normals_s[a] = jnp.concatenate(
            [-(geometry[DOF + d, a : a + 1, :] * root) for d in range(DOF)] + [zero1] * 2, axis=0
        )
        half = [knot_par[a : a + 1, :].astype(F32), spline[1, a : a + 1, :], rho, zero1]
        info_s[a] = jnp.concatenate(half + half, axis=0)
        match_s[a] = jnp.broadcast_to(match[a : a + 1, :], (SUB, LANES))
    row = iota((SUB, LANES), 0)
    for j in range(lanes):
        normals = []
        infos = []
        flags = []
        for r in range(CAP):
            e = filled[2 * j + r]
            safe = jnp.maximum(e, 0)
            a = jnp.right_shift(safe, 2)
            m = jnp.where(e < 0, -1, jnp.bitwise_and(safe, 3))
            pick = picks[lane * drives + a, jnp.bitwise_and(safe, 3)]
            there = jnp.logical_and(e >= 0, counts[a] > street * LANES)
            flags.append(jnp.where(there, pick + 1, 0).astype(F32))
            normals.append(jnp.where(match_s[a] == m, normals_s[a], 0.0))
            infos.append(info_s[a])
        info = jnp.where(row < 4, infos[0], infos[1])
        info = jnp.where(row == 3, flags[0], jnp.where(row == 7, flags[1], info))
        for t in range(street_size):
            send[j, t, 0:SUB, :] = normals[0]
            send[j, t, SUB : 2 * SUB, :] = normals[1]
            send[j, t, 2 * SUB : 3 * SUB, :] = info


def put_values(out_ref, tab, own_ref, inc_ref, lst, tiles_ref):
    street_size, drives = own_ref.shape[0], own_ref.shape[1]
    entries = drives * MATCH
    for a in range(drives):
        tiles = [tiles_ref[a, h] for h in range(HIGH)]
        for s in range(street_size):
            normals, knot, basis, _ = own_tile(own_ref, s, a)
            value = gather_value(tiles, knot, basis, normals)
            for m in range(MATCH):
                e = a * MATCH + m
                out_ref[tab[e], pl.ds(tab[entries + e] * street_size + s, 1), :] = value

    def one(code):
        pick, rank, block, lane, part = decode(code, street_size)
        normals, knot, basis, _ = inc_tile(inc_ref, block, rank)
        value = gather_value([tiles_ref[pick, h] for h in range(HIGH)], knot, basis, normals)
        out_ref[lane, pl.ds((CAP + rank) * street_size + part, 1), :] = value

    count = lst[lst.shape[0] - 1]

    def two(i, carry):
        one(lst[2 * i])
        one(lst[2 * i + 1])
        return carry

    lax.fori_loop(0, jnp.right_shift(count + 1, 1), two, 0)


def own_sum(sent, got, tab, a, s, street_size, entries):
    e = a * MATCH
    total = sent[tab[e], pl.ds(tab[entries + e] * street_size + s, 1), :]
    for m in range(MATCH):
        e = a * MATCH + m
        total = total + got[tab[e], pl.ds((CAP + tab[entries + e]) * street_size + s, 1), :]
    return total


def inc_sum(sent, got, rank, lane, part, street_size):
    return (
        got[lane, pl.ds(rank * street_size + part, 1), :]
        + sent[lane, pl.ds((CAP + rank) * street_size + part, 1), :]
    )


def spread_all(acc, own_ref, inc_ref, lst, kinds_own, kinds_inc):
    street_size, drives = own_ref.shape[0], own_ref.shape[1]
    for a in range(drives):
        total = None
        for s in range(street_size):
            normals, knot, basis, rho = own_tile(own_ref, s, a)
            coeffs = [basis[k] * normals for k in range(4)]
            part = spread(knot, kinds_own(coeffs, rho, a, s))
            total = part if total is None else total + part
        acc[a] = total

    count = lst[lst.shape[0] - 1]

    def one(index):
        pick, rank, block, lane, part = decode(lst[index], street_size)
        normals, knot, basis, rho = inc_tile(inc_ref, block, rank)
        normals = jnp.where(index < count, normals, 0.0)
        coeffs = [basis[k] * normals for k in range(4)]
        return pick, spread(knot, kinds_inc(coeffs, rho, rank, lane, part))

    def two(i, carry):
        first = one(2 * i)
        second = one(2 * i + 1)
        for pick, value in (first, second):
            acc[pick] = acc[pick] + value
        return carry

    lax.fori_loop(0, jnp.right_shift(count + 1, 1), two, 0)


def start_kernel(tab, own, inc, grad, diag, direction, out, lst, acc):
    drives = own.shape[1]
    blocks = inc.shape[0]
    count = 0
    for b in range(blocks):
        flags = inc[b, 2 * SUB : 3 * SUB, :].astype(jnp.int32)
        for r in range(CAP):
            flag = flags[4 * r + 3, 0]
            lst[count] = (b * CAP + r) * 4 + flag - 1
            count = count + jnp.where(flag > 0, 1, 0)
    lst[count] = lst[jnp.maximum(count - 1, 0)]
    lst[lst.shape[0] - 1] = count

    def kinds(coeffs, rho, *_):
        return [[c * rho for c in coeffs], [c * c for c in coeffs]]

    spread_all(acc, own, inc, lst, kinds, kinds)
    for a in range(drives):
        sums = acc[a]
        gradient = fold_shifts(sums, 0)
        squares = fold_shifts(sums, 128)
        for h in range(HIGH):
            diagonal = 1.0 + squares[h]
            grad[a, h] = gradient[h]
            diag[a, h] = diagonal
            direction[a, h] = gradient[h] / diagonal
    out[...] = jnp.zeros(out.shape, F32)
    put_values(out, tab, own, inc, lst, direction)


def scalar_row(values):
    lane = iota((1, LANES), 1)
    row = jnp.zeros((1, LANES), F32)
    for i, value in enumerate(values):
        total = jnp.sum(jnp.sum(value, axis=0, keepdims=True), axis=1, keepdims=True)
        row = jnp.where(lane == i, total, row)
    return row


def pick_lane(row, i):
    return jnp.sum(jnp.where(iota((1, LANES), 1) == i, row, 0.0), axis=1, keepdims=True)


def middle_kernel(
    tab, lst, own, inc, grad, diag, direction, sent, got, image, values, out, acc, ratio
):
    street_size, drives = own.shape[0], own.shape[1]
    entries = drives * MATCH
    for a in range(drives):
        for s in range(street_size):
            values[pl.ds(s * drives + a, 1), :] = own_sum(sent, got, tab, a, s, street_size, entries)

    def kinds_own(coeffs, rho, a, s):
        value = jnp.broadcast_to(values[pl.ds(s * drives + a, 1), :], (SUB, LANES))
        return [[c * value for c in coeffs]]

    def kinds_inc(coeffs, rho, rank, lane, part):
        value = inc_sum(sent, got, rank, lane, part, street_size)
        value = jnp.broadcast_to(value, (SUB, LANES))
        return [[c * value for c in coeffs]]

    spread_all(acc, own, inc, lst, kinds_own, kinds_inc)
    first = jnp.zeros((SUB, LANES), F32)
    second = jnp.zeros((SUB, LANES), F32)
    for a in range(drives):
        sums = fold_shifts(acc[a], 0)
        for h in range(HIGH):
            p = direction[a, h]
            q = p + sums[h]
            image[a, h] = q
            ratio[a, h] = q / diag[a, h]
            first = first + grad[a, h] * p
            second = second + p * q
    out[...] = jnp.zeros(out.shape, F32)
    put_values(out, tab, own, inc, lst, ratio)
    row = scalar_row([first, second])
    rows = 2 * CAP * street_size
    for j in range(out.shape[0]):
        out[j, rows : rows + 1, :] = row


def dots_kernel(tab, grad, diag, direction, image, values, sent, got, resid, precond, steps, out):
    drives = grad.shape[0]
    street_size = values.shape[0] // drives
    entries = drives * MATCH
    rows = 2 * CAP * street_size
    total = got[0, rows : rows + 1, :]
    for j in range(1, got.shape[0]):
        total = total + got[j, rows : rows + 1, :]
    inner = pick_lane(total, 0)
    curve = pick_lane(total, 1)
    alpha = inner / curve
    one = jnp.zeros((SUB, LANES), F32)
    two = jnp.zeros((SUB, LANES), F32)
    three = jnp.zeros((SUB, LANES), F32)
    for a in range(drives):
        for h in range(HIGH):
            r = grad[a, h] - alpha * image[a, h]
            z = r / diag[a, h]
            resid[a, h] = r
            precond[a, h] = z
            one = one + r * z
            two = two + z * z
            three = three + z * direction[a, h]
    slots2 = jnp.zeros((1, LANES), F32)
    slots3 = jnp.zeros((1, LANES), F32)
    for a in range(drives):
        for s in range(street_size):
            before = values[pl.ds(s * drives + a, 1), :]
            value = before - alpha * own_sum(sent, got, tab, a, s, street_size, entries)
            slots2 = slots2 + value * value
            slots3 = slots3 + value * before
    head = iota((SUB, LANES), 0) == 0
    two = two + jnp.where(head, jnp.broadcast_to(slots2, (SUB, LANES)), 0.0)
    three = three + jnp.where(head, jnp.broadcast_to(slots3, (SUB, LANES)), 0.0)
    row = jnp.broadcast_to(scalar_row([one, two, three]), (SUB, LANES))
    for j in range(out.shape[0]):
        out[j] = row
    lane = iota((SUB, LANES), 1)
    steps[...] = jnp.where(lane == 0, alpha, jnp.where(lane == 1, inner, curve))


def last_kernel(
    meta, tab, lst, own, inc, direction, image, values, sent, got, sent2, got2, resid, precond,
    steps, o_p, o_z, o_r, o_h, o_q, acc, hess,
):
    street_size, drives = own.shape[0], own.shape[1]
    entries = drives * MATCH
    alpha = steps[0:1, 0:1]

    def kinds_own(coeffs, rho, a, s):
        value = values[pl.ds(s * drives + a, 1), :] - alpha * own_sum(
            sent2, got2, tab, a, s, street_size, entries
        )
        value = jnp.broadcast_to(value, (SUB, LANES))
        return [[c * value for c in coeffs]]

    def kinds_inc(coeffs, rho, rank, lane, part):
        value = inc_sum(sent, got, rank, lane, part, street_size) - alpha * inc_sum(
            sent2, got2, rank, lane, part, street_size
        )
        value = jnp.broadcast_to(value, (SUB, LANES))
        return [[c * value for c in coeffs]]

    spread_all(acc, own, inc, lst, kinds_own, kinds_inc)
    for a in range(drives):
        sums = fold_shifts(acc[a], 0)
        for h in range(HIGH):
            hess[a, h] = precond[a, h] + sums[h]
    blocks = o_p.shape[1]
    tiles = PARAMS // LANES
    row = iota((SUB, LANES), 0)
    points = []
    masks = []
    for q in range(tiles):
        entry = q * LANES + iota((SUB, LANES), 1)
        point = jnp.right_shift(entry * 10923, 16)
        points.append(point)
        masks.append(row == entry - point * DOF)
    for bl in range(blocks):
        block = meta[1] * blocks + bl
        high = jnp.right_shift(block, 1)
        offset = jnp.bitwise_and(block, 1) * (LANES // 2)
        indices = [offset + points[q] for q in range(tiles)]
        for a in range(drives):
            for source, target in (
                (direction, o_p), (precond, o_z), (resid, o_r), (hess, o_h), (image, o_q)
            ):
                tile = source[a, high]
                for q in range(tiles):
                    value = jnp.where(masks[q], take_lanes(tile, indices[q]), 0.0)
                    target[a, bl : bl + 1, q * LANES : (q + 1) * LANES] = jnp.sum(
                        value, axis=0, keepdims=True
                    )


def finish_kernel(steps, got, o_p, o_z, o_r, o_h, o_q, step_out, resid_out):
    total = got[0]
    for j in range(1, got.shape[0]):
        total = total + got[j]
    total = total[0:1, :]
    inner_next = pick_lane(total, 0)
    alpha = steps[0:1, 0:1]
    inner = steps[0:1, 1:2]
    curve = steps[0:1, 2:3]
    beta = inner_next / inner
    denominator = pick_lane(total, 1) + 2.0 * beta * pick_lane(total, 2) + beta * beta * curve
    last = inner_next / denominator
    for a in range(o_p.shape[0]):
        p = o_p[a]
        step_out[a] = alpha * p + last * (o_z[a] + beta * p)
        resid_out[a] = o_r[a] - last * (o_h[a] + beta * o_q[a])


def call(kernel, shapes, spaces_in, spaces_out, scratch=(), **kwargs):
    where = {"s": pltpu.SMEM, "v": pltpu.VMEM}
    return pl.pallas_call(
        kernel,
        out_shape=[jax.ShapeDtypeStruct(s, d) for s, d in shapes],
        in_specs=[pl.BlockSpec(memory_space=where[c]) for c in spaces_in],
        out_specs=[pl.BlockSpec(memory_space=where[c]) for c in spaces_out],
        scratch_shapes=list(scratch),
        compiler_params=pltpu.CompilerParams(vmem_limit_bytes=40 * 1024 * 1024),
        **kwargs,
    )


def body(
    pt_count,
    partner_dev,
    partner_pick,
    knot_own,
    knot_partner,
    match_slot,
    spline,
    geometry,
    point_weight,
    point_resid,
):
    drives = knot_own.shape[0]
    lanes = lax.axis_size("drive")
    street_size = lax.axis_size("street")
    meta = jnp.stack([lax.axis_index("drive"), lax.axis_index("street")]).astype(jnp.int32)
    entries = drives * MATCH
    blocks = lanes * street_size
    param = ((drives, HIGH, SUB, LANES), F32)
    send, mine, tab = call(
        send_kernel,
        [
            ((lanes, street_size, 3 * SUB, LANES), F32),
            ((drives, 2 * SUB, LANES), F32),
            ((2 * entries,), jnp.int32),
        ],
        "ssssvvvvvvv",
        "vvs",
        [
            pltpu.SMEM((CAP * lanes,), jnp.int32),
            pltpu.SMEM((lanes,), jnp.int32),
            pltpu.VMEM((drives, SUB, LANES), F32),
            pltpu.VMEM((drives, SUB, LANES), F32),
            pltpu.VMEM((drives, SUB, LANES), jnp.int32),
        ],
        name="send",
    )(
        meta, pt_count, partner_dev, partner_pick, knot_own, knot_partner, match_slot,
        spline, geometry, point_weight, point_resid,
    )
    if street_size == 2:
        peer = lax.ppermute(mine, "street", [(0, 1), (1, 0)])
        first = meta[1] == 0
        own = jnp.stack([jnp.where(first, mine, peer), jnp.where(first, peer, mine)])
    else:
        own = lax.all_gather(mine, "street", axis=0, tiled=False)
    inc = lax.all_to_all(
        send.reshape(blocks, 3 * SUB, LANES), ("drive", "street"), split_axis=0, concat_axis=0, tiled=True
    )
    exchange = ((lanes, 2 * CAP * street_size, LANES), F32)
    exchange2 = ((lanes, 2 * CAP * street_size + SUB, LANES), F32)
    acc = pltpu.VMEM((drives, 128, LANES), F32)
    list_size = CAP * blocks + 2
    grad, diag, direction, sent, lst = call(
        start_kernel,
        [param, param, param, exchange, ((list_size,), jnp.int32)],
        "svv",
        "vvvvs",
        [pltpu.VMEM((drives, 256, LANES), F32)],
        name="start",
    )(tab, own, inc)
    got = lax.all_to_all(sent, "drive", split_axis=0, concat_axis=0, tiled=True)
    image, values, sent2 = call(
        middle_kernel,
        [param, ((street_size * drives, LANES), F32), exchange2],
        "ssvvvvvvv",
        "vvv",
        [acc, pltpu.VMEM(param[0], F32)],
        name="middle",
    )(tab, lst, own, inc, grad, diag, direction, sent, got)
    got2 = lax.all_to_all(sent2, "drive", split_axis=0, concat_axis=0, tiled=True)
    resid, precond, steps, sent3 = call(
        dots_kernel,
        [param, param, ((SUB, LANES), F32), ((lanes, SUB, LANES), F32)],
        "svvvvvvv",
        "vvvv",
        name="dots",
    )(tab, grad, diag, direction, image, values, sent2, got2)
    got3 = lax.all_to_all(sent3, "drive", split_axis=0, concat_axis=0, tiled=True)
    shape = ((drives, NBLK // street_size, PARAMS), F32)
    parts = call(
        last_kernel,
        [shape] * 5,
        "sssvvvvvvvvvvvv",
        "vvvvv",
        [acc, pltpu.VMEM(param[0], F32)],
        name="last",
        cost_estimate=pl.CostEstimate(flops=200000000, bytes_accessed=8000000, transcendentals=0),
    )(meta, tab, lst, own, inc, direction, image, values, sent, got, sent2, got2, resid, precond, steps)
    return tuple(
        call(finish_kernel, [shape, shape], "vvvvvvv", "vv", name="finish")(steps, got3, *parts)
    )


def solution(mesh):
    placed = (
        P(("region", "drive")),
        P("region", None),
        P("region", None),
        P(("region", "drive"), "street"),
        P(("region", "drive"), "street"),
        P(("region", "drive"), "street"),
        P(None, ("region", "drive"), "street"),
        P(None, ("region", "drive"), "street"),
        P(("region", "drive"), "street"),
        P(("region", "drive"), "street"),
    )
    return jax.shard_map(
        body,
        mesh=mesh,
        in_specs=placed,
        out_specs=(P(("region", "drive"), "street", None), P(("region", "drive"), "street", None)),
        check_vma=False,
    )
```

```python
import jax
import jax.numpy as jnp
from jax import lax
from jax.experimental import pallas as pl
from jax.experimental.pallas import tpu as pltpu
from jax.sharding import PartitionSpec as P

NBLK = 8
DOF = 6
PARAMS = 384
MATCH = 4
LANES = 128
HIGH = 4
CAP = 2
SUB = 8
UNROLL = 4
F32 = jnp.float32
BF16 = jnp.bfloat16


def iota(shape, dim):
    return lax.broadcasted_iota(jnp.int32, shape, dim)


def take_lanes(values, index):
    return jnp.take_along_axis(values, index, axis=1, mode="promise_in_bounds")


def row_of(block, row, count=SUB):
    return jnp.broadcast_to(block[row : row + 1, :], (count, LANES))


def basis_of(s):
    remain = 1.0 - s
    square = s * s
    cube = square * s
    return (
        remain * remain * remain * (1.0 / 6.0),
        (3.0 * cube - 6.0 * square + 4.0) * (1.0 / 6.0),
        (-3.0 * cube + 3.0 * square + 3.0 * s + 1.0) * (1.0 / 6.0),
        cube * (1.0 / 6.0),
    )


def split_two(values):
    high = values.astype(BF16)
    low = (values - high.astype(F32)).astype(BF16)
    return jnp.concatenate([high, low], axis=1)


def places():
    return iota((LANES, LANES), 0).astype(F32).astype(BF16)


def spread(place, knot, kinds):
    low = jnp.bitwise_and(knot, LANES - 1).astype(F32)
    high = jnp.right_shift(knot, 7)
    low = jnp.concatenate([low, low], axis=0).astype(BF16)
    low = jnp.concatenate([low] * (LANES // 16), axis=0)
    hot = jnp.where(place == low, jnp.ones((), BF16), jnp.zeros((), BF16))
    hot = jnp.concatenate([hot, hot], axis=1)
    masks = []
    for h in range(HIGH):
        mask = jnp.where(high == h, 1.0, 0.0)
        mask = jnp.concatenate([mask, mask], axis=0).astype(BF16)
        mask = jnp.concatenate([mask, mask], axis=0)
        masks.append(jnp.concatenate([mask, mask], axis=1))
    rows = []
    for kind in kinds:
        parts = split_two(jnp.concatenate(kind, axis=0))
        for h in range(HIGH):
            rows.append(parts * masks[h])
    left = jnp.concatenate(rows, axis=0)
    return lax.dot_general(left, hot, (((1,), (1,)), ((), ())), preferred_element_type=F32)


def fold_shifts(acc, base):
    lane = iota((SUB, LANES), 1)
    out = []
    before = None
    for h in range(HIGH):
        tiles = [acc[base + h * 32 + k * SUB : base + h * 32 + (k + 1) * SUB, :] for k in range(4)]
        rolled = [None] + [pltpu.roll(tiles[k], k, axis=1) for k in range(1, 4)]
        total = tiles[0]
        for k in range(1, 4):
            other = before[k] if before is not None else jnp.zeros((SUB, LANES), F32)
            total = total + jnp.where(lane >= k, rolled[k], other)
        out.append(total)
        before = rolled
    return out


def gather_value(tiles, knot, basis, normals):
    total = None
    for k in range(4):
        index = knot + k
        low = jnp.bitwise_and(index, LANES - 1)
        high = jnp.right_shift(index, 7)
        value = take_lanes(tiles[HIGH - 1], low)
        for h in range(HIGH - 1):
            value = jnp.where(high == h, take_lanes(tiles[h], low), value)
        term = basis[k] * value
        total = term if total is None else total + term
    return jnp.sum(normals * total, axis=0, keepdims=True)


def own_tile(own_ref, h, a):
    normals = own_ref[h, a, 0:SUB, :]
    info = own_ref[h, a, SUB : 2 * SUB, :]
    return normals, row_of(info, 0).astype(jnp.int32), basis_of(row_of(info, 1)), row_of(info, 2)


def inc_tile(inc_ref, block, rank):
    tile = jnp.concatenate([inc_ref[block, 2 * rank], inc_ref[block, 2 * rank + 1]], axis=0)
    info = inc_ref[block, 4]
    knot = jnp.where(rank == 0, info[0:1], info[1:2])
    normals = jnp.where(iota((SUB, LANES), 0) < DOF, tile, 0.0)
    knot = jnp.broadcast_to(knot, (SUB, LANES)).astype(jnp.int32)
    return normals, knot, basis_of(row_of(tile, 6)), row_of(tile, 7)


def decode(code, street_size):
    pick = jnp.bitwise_and(code, 3)
    tile = jnp.right_shift(code, 2)
    rank = jnp.bitwise_and(tile, 1)
    block = jnp.right_shift(tile, 1)
    lane = lax.div(block, street_size)
    part = block - lane * street_size
    return pick, rank, block, lane, part


def send_kernel(
    meta, counts, dev, picks, knot_own, knot_par, match, spline, geometry, weight, resid,
    send, own, tab, filled, taken, normals_s, knots_s, match_s,
):
    drives = counts.shape[0]
    lanes = send.shape[0]
    street_size = send.shape[1]
    lane = meta[0]
    street = meta[1]
    for j in range(lanes):
        taken[j] = 0
        filled[2 * j] = -1
        filled[2 * j + 1] = -1
    for a in range(drives):
        for m in range(MATCH):
            e = a * MATCH + m
            dest = dev[m, lane * drives + a]
            rank = taken[dest]
            taken[dest] = rank + 1
            tab[e] = dest
            tab[drives * MATCH + e] = rank
            filled[2 * dest + rank] = e
    slot = street * LANES + iota((1, LANES), 1)
    zero1 = jnp.zeros((1, LANES), F32)
    for a in range(drives):
        w = jnp.where(slot < counts[a], weight[a : a + 1, :], 0.0)
        root = jnp.sqrt(w)
        rho = -(root * resid[a : a + 1, :])
        own[a, 0:SUB, :] = jnp.concatenate(
            [geometry[d, a : a + 1, :] * root for d in range(DOF)] + [zero1] * 2, axis=0
        )
        own[a, SUB : 2 * SUB, :] = jnp.concatenate(
            [knot_own[a : a + 1, :].astype(F32), spline[0, a : a + 1, :], rho] + [zero1] * 5, axis=0
        )
        normals_s[a] = jnp.concatenate(
            [-(geometry[DOF + d, a : a + 1, :] * root) for d in range(DOF)]
            + [spline[1, a : a + 1, :], rho],
            axis=0,
        )
        knots_s[a] = jnp.broadcast_to(knot_par[a : a + 1, :].astype(F32), (4, LANES))
        match_s[a] = jnp.broadcast_to(match[a : a + 1, :], (SUB, LANES))
    row = iota((4, LANES), 0)
    for j in range(lanes):
        normals = []
        infos = []
        flags = []
        for r in range(CAP):
            e = filled[2 * j + r]
            safe = jnp.maximum(e, 0)
            a = jnp.right_shift(safe, 2)
            m = jnp.where(e < 0, -1, jnp.bitwise_and(safe, 3))
            pick = picks[jnp.bitwise_and(safe, 3), lane * drives + a]
            there = jnp.logical_and(e >= 0, counts[a] > street * LANES)
            flags.append(jnp.where(there, pick + 1, 0).astype(F32))
            normals.append(jnp.where(match_s[a] == m, normals_s[a], 0.0))
            infos.append(knots_s[a])
        info = jnp.where(row == 0, infos[0], infos[1])
        info = jnp.where(row == 2, flags[0], jnp.where(row == 3, flags[1], info))
        for t in range(street_size):
            for r in range(CAP):
                send[j, t, 2 * r] = normals[r][0:4]
                send[j, t, 2 * r + 1] = normals[r][4:8]
            send[j, t, 4] = info


def put_values(out_ref, tab, own_ref, inc_ref, lst, tiles_ref):
    street_size, drives = own_ref.shape[0], own_ref.shape[1]
    entries = drives * MATCH
    for a in range(drives):
        tiles = [tiles_ref[a, h] for h in range(HIGH)]
        for s in range(street_size):
            normals, knot, basis, _ = own_tile(own_ref, s, a)
            value = gather_value(tiles, knot, basis, normals)
            for m in range(MATCH):
                e = a * MATCH + m
                out_ref[tab[e], tab[entries + e] * street_size + s] = value

    def one(code):
        pick, rank, block, lane, part = decode(code, street_size)
        normals, knot, basis, _ = inc_tile(inc_ref, block, rank)
        value = gather_value([tiles_ref[pick, h] for h in range(HIGH)], knot, basis, normals)
        out_ref[lane, (CAP + rank) * street_size + part] = value

    count = lst[lst.shape[0] - 1]

    def some(i, carry):
        for j in range(UNROLL):
            one(lst[UNROLL * i + j])
        return carry

    lax.fori_loop(0, lax.div(count + UNROLL - 1, UNROLL), some, 0)


def own_sum(sent, got, tab, a, s, street_size, entries):
    e = a * MATCH
    total = sent[tab[e], tab[entries + e] * street_size + s]
    for m in range(MATCH):
        e = a * MATCH + m
        total = total + got[tab[e], (CAP + tab[entries + e]) * street_size + s]
    return total


def inc_sum(sent, got, rank, lane, part, street_size):
    return (
        got[lane, rank * street_size + part]
        + sent[lane, (CAP + rank) * street_size + part]
    )


def spread_own(acc, own_ref, kinds_own):
    street_size, drives = own_ref.shape[0], own_ref.shape[1]
    place = places()
    for a in range(drives):
        total = None
        for s in range(street_size):
            normals, knot, basis, rho = own_tile(own_ref, s, a)
            coeffs = [basis[k] * normals for k in range(4)]
            part = spread(place, knot, kinds_own(coeffs, rho, a, s))
            total = part if total is None else total + part
        acc[a] = total


def spread_inc(acc, street_size, inc_ref, lst, kinds_inc):
    place = places()
    count = lst[lst.shape[0] - 1]

    def one(index):
        pick, rank, block, lane, part = decode(lst[index], street_size)
        normals, knot, basis, rho = inc_tile(inc_ref, block, rank)
        normals = jnp.where(index < count, normals, 0.0)
        coeffs = [basis[k] * normals for k in range(4)]
        return pick, spread(place, knot, kinds_inc(coeffs, rho, rank, lane, part))

    def some(i, carry):
        for pick, value in [one(UNROLL * i + j) for j in range(UNROLL)]:
            acc[pick] = acc[pick] + value
        return carry

    lax.fori_loop(0, lax.div(count + UNROLL - 1, UNROLL), some, 0)


def start_kinds(coeffs, rho, *_):
    return [[c * rho for c in coeffs], [c * c for c in coeffs]]


def own_kernel(own, acc):
    spread_own(acc, own, start_kinds)


def start_kernel(tab, own, inc, begun, grad, diag, direction, out, lst, acc):
    drives = own.shape[1]
    street_size = own.shape[0]
    blocks = inc.shape[0]
    count = 0
    for b in range(blocks):
        flags = inc[b, 4].astype(jnp.int32)
        for r in range(CAP):
            flag = flags[2 + r, 0]
            lst[count] = (b * CAP + r) * 4 + flag - 1
            count = count + jnp.where(flag > 0, 1, 0)
    last = lst[jnp.maximum(count - 1, 0)]
    for i in range(UNROLL - 1):
        lst[count + i] = last
    lst[lst.shape[0] - 1] = count

    acc[...] = begun[...]
    spread_inc(acc, street_size, inc, lst, start_kinds)
    for a in range(drives):
        sums = acc[a]
        gradient = fold_shifts(sums, 0)
        squares = fold_shifts(sums, 128)
        for h in range(HIGH):
            diagonal = 1.0 + squares[h]
            grad[a, h] = gradient[h]
            diag[a, h] = diagonal
            direction[a, h] = gradient[h] / diagonal
    out[...] = jnp.zeros(out.shape, F32)
    put_values(out, tab, own, inc, lst, direction)


def scalar_row(values):
    lane = iota((1, LANES), 1)
    row = jnp.zeros((1, LANES), F32)
    for i, value in enumerate(values):
        total = jnp.sum(jnp.sum(value, axis=0, keepdims=True), axis=1, keepdims=True)
        row = jnp.where(lane == i, total, row)
    return row


def pick_lane(row, i):
    return jnp.sum(jnp.where(iota((1, LANES), 1) == i, row, 0.0), axis=1, keepdims=True)


def middle_kernel(
    tab, lst, own, inc, grad, diag, direction, sent, got, image, values, out, acc, ratio
):
    street_size, drives = own.shape[0], own.shape[1]
    entries = drives * MATCH
    for a in range(drives):
        for s in range(street_size):
            values[pl.ds(s * drives + a, 1), :] = own_sum(sent, got, tab, a, s, street_size, entries)

    def kinds_own(coeffs, rho, a, s):
        value = jnp.broadcast_to(values[pl.ds(s * drives + a, 1), :], (SUB, LANES))
        return [[c * value for c in coeffs]]

    def kinds_inc(coeffs, rho, rank, lane, part):
        value = inc_sum(sent, got, rank, lane, part, street_size)
        value = jnp.broadcast_to(value, (SUB, LANES))
        return [[c * value for c in coeffs]]

    spread_own(acc, own, kinds_own)
    spread_inc(acc, street_size, inc, lst, kinds_inc)
    first = jnp.zeros((SUB, LANES), F32)
    second = jnp.zeros((SUB, LANES), F32)
    for a in range(drives):
        sums = fold_shifts(acc[a], 0)
        for h in range(HIGH):
            p = direction[a, h]
            q = p + sums[h]
            image[a, h] = q
            ratio[a, h] = q / diag[a, h]
            first = first + grad[a, h] * p
            second = second + p * q
    out[...] = jnp.zeros(out.shape, F32)
    put_values(out, tab, own, inc, lst, ratio)
    row = scalar_row([first, second])
    rows = 2 * CAP * street_size
    for j in range(out.shape[0]):
        out[j, rows] = row


def dots_kernel(tab, grad, diag, direction, image, values, sent, got, resid, precond, steps, out):
    drives = grad.shape[0]
    street_size = values.shape[0] // drives
    entries = drives * MATCH
    rows = 2 * CAP * street_size
    total = got[0, rows]
    for j in range(1, got.shape[0]):
        total = total + got[j, rows]
    inner = pick_lane(total, 0)
    curve = pick_lane(total, 1)
    alpha = inner / curve
    one = jnp.zeros((SUB, LANES), F32)
    two = jnp.zeros((SUB, LANES), F32)
    three = jnp.zeros((SUB, LANES), F32)
    for a in range(drives):
        for h in range(HIGH):
            r = grad[a, h] - alpha * image[a, h]
            z = r / diag[a, h]
            resid[a, h] = r
            precond[a, h] = z
            one = one + r * z
            two = two + z * z
            three = three + z * direction[a, h]
    slots2 = jnp.zeros((1, LANES), F32)
    slots3 = jnp.zeros((1, LANES), F32)
    for a in range(drives):
        for s in range(street_size):
            before = values[pl.ds(s * drives + a, 1), :]
            value = before - alpha * own_sum(sent, got, tab, a, s, street_size, entries)
            slots2 = slots2 + value * value
            slots3 = slots3 + value * before
    head = iota((SUB, LANES), 0) == 0
    two = two + jnp.where(head, jnp.broadcast_to(slots2, (SUB, LANES)), 0.0)
    three = three + jnp.where(head, jnp.broadcast_to(slots3, (SUB, LANES)), 0.0)
    row = jnp.broadcast_to(scalar_row([one, two, three]), (SUB, LANES))
    for j in range(out.shape[0]):
        out[j] = row
    lane = iota((SUB, LANES), 1)
    steps[...] = jnp.where(lane == 0, alpha, jnp.where(lane == 1, inner, curve))


def last_kernel(
    meta, tab, lst, own, inc, direction, image, values, sent, got, sent2, got2, resid, precond,
    steps, o_p, o_z, o_r, o_h, o_q, acc, hess,
):
    street_size, drives = own.shape[0], own.shape[1]
    entries = drives * MATCH
    alpha = steps[0:1, 0:1]

    def kinds_own(coeffs, rho, a, s):
        value = values[pl.ds(s * drives + a, 1), :] - alpha * own_sum(
            sent2, got2, tab, a, s, street_size, entries
        )
        value = jnp.broadcast_to(value, (SUB, LANES))
        return [[c * value for c in coeffs]]

    def kinds_inc(coeffs, rho, rank, lane, part):
        value = inc_sum(sent, got, rank, lane, part, street_size) - alpha * inc_sum(
            sent2, got2, rank, lane, part, street_size
        )
        value = jnp.broadcast_to(value, (SUB, LANES))
        return [[c * value for c in coeffs]]

    spread_own(acc, own, kinds_own)
    spread_inc(acc, street_size, inc, lst, kinds_inc)
    for a in range(drives):
        sums = fold_shifts(acc[a], 0)
        for h in range(HIGH):
            hess[a, h] = precond[a, h] + sums[h]
    blocks = o_p.shape[1]
    tiles = PARAMS // LANES
    row = iota((SUB, LANES), 0)
    points = []
    masks = []
    for q in range(tiles):
        entry = q * LANES + iota((SUB, LANES), 1)
        point = jnp.right_shift(entry * 10923, 16)
        points.append(point)
        masks.append(row == entry - point * DOF)
    for bl in range(blocks):
        block = meta[1] * blocks + bl
        high = jnp.right_shift(block, 1)
        offset = jnp.bitwise_and(block, 1) * (LANES // 2)
        indices = [offset + points[q] for q in range(tiles)]
        for a in range(drives):
            for source, target in (
                (direction, o_p), (precond, o_z), (resid, o_r), (hess, o_h), (image, o_q)
            ):
                tile = source[a, high]
                for q in range(tiles):
                    value = jnp.where(masks[q], take_lanes(tile, indices[q]), 0.0)
                    target[a, bl : bl + 1, q * LANES : (q + 1) * LANES] = jnp.sum(
                        value, axis=0, keepdims=True
                    )


def finish_kernel(steps, got, o_p, o_z, o_r, o_h, o_q, step_out, resid_out):
    total = got[0]
    for j in range(1, got.shape[0]):
        total = total + got[j]
    total = total[0:1, :]
    inner_next = pick_lane(total, 0)
    alpha = steps[0:1, 0:1]
    inner = steps[0:1, 1:2]
    curve = steps[0:1, 2:3]
    beta = inner_next / inner
    denominator = pick_lane(total, 1) + 2.0 * beta * pick_lane(total, 2) + beta * beta * curve
    last = inner_next / denominator
    for a in range(o_p.shape[0]):
        p = o_p[a]
        step_out[a] = alpha * p + last * (o_z[a] + beta * p)
        resid_out[a] = o_r[a] - last * (o_h[a] + beta * o_q[a])


def call(kernel, shapes, spaces_in, spaces_out, scratch=(), **kwargs):
    where = {"s": pltpu.SMEM, "v": pltpu.VMEM}
    return pl.pallas_call(
        kernel,
        out_shape=[jax.ShapeDtypeStruct(s, d) for s, d in shapes],
        in_specs=[pl.BlockSpec(memory_space=where[c]) for c in spaces_in],
        out_specs=[pl.BlockSpec(memory_space=where[c]) for c in spaces_out],
        scratch_shapes=list(scratch),
        compiler_params=pltpu.CompilerParams(vmem_limit_bytes=40 * 1024 * 1024),
        **kwargs,
    )


def body(
    pt_count,
    partner_dev,
    partner_pick,
    knot_own,
    knot_partner,
    match_slot,
    spline,
    geometry,
    point_weight,
    point_resid,
):
    drives = knot_own.shape[0]
    lanes = lax.axis_size("drive")
    street_size = lax.axis_size("street")
    meta = jnp.stack([lax.axis_index("drive"), lax.axis_index("street")]).astype(jnp.int32)
    entries = drives * MATCH
    blocks = lanes * street_size
    param = ((drives, HIGH, SUB, LANES), F32)
    send, mine, tab = call(
        send_kernel,
        [
            ((lanes, street_size, 5, 4, LANES), F32),
            ((drives, 2 * SUB, LANES), F32),
            ((2 * entries,), jnp.int32),
        ],
        "ssssvvvvvvv",
        "vvs",
        [
            pltpu.SMEM((CAP * lanes,), jnp.int32),
            pltpu.SMEM((lanes,), jnp.int32),
            pltpu.VMEM((drives, SUB, LANES), F32),
            pltpu.VMEM((drives, 4, LANES), F32),
            pltpu.VMEM((drives, SUB, LANES), jnp.int32),
        ],
        name="send",
    )(
        meta, pt_count, partner_dev.T, partner_pick.T, knot_own, knot_partner, match_slot,
        spline, geometry, point_weight, point_resid,
    )
    if street_size == 2:
        peer = lax.ppermute(mine, "street", [(0, 1), (1, 0)])
        first = meta[1] == 0
        own = jnp.stack([jnp.where(first, mine, peer), jnp.where(first, peer, mine)])
    else:
        own = lax.all_gather(mine, "street", axis=0, tiled=False)
    inc = lax.all_to_all(
        send.reshape(blocks, 5, 4, LANES), ("drive", "street"), split_axis=0, concat_axis=0, tiled=True
    )
    exchange = ((lanes, 2 * CAP * street_size, 1, LANES), F32)
    exchange2 = ((lanes, 2 * CAP * street_size + 1, 1, LANES), F32)
    acc = pltpu.VMEM((drives, 128, LANES), F32)
    list_size = CAP * blocks + UNROLL
    (begun,) = call(
        own_kernel,
        [((drives, 256, LANES), F32)],
        "v",
        "v",
        name="own",
        cost_estimate=pl.CostEstimate(flops=70000000, bytes_accessed=1000000, transcendentals=0),
    )(own)
    grad, diag, direction, sent, lst = call(
        start_kernel,
        [param, param, param, exchange, ((list_size,), jnp.int32)],
        "svvv",
        "vvvvs",
        [pltpu.VMEM((drives, 256, LANES), F32)],
        name="start",
    )(tab, own, inc, begun)
    got = lax.all_to_all(sent, "drive", split_axis=0, concat_axis=0, tiled=True)
    image, values, sent2 = call(
        middle_kernel,
        [param, ((street_size * drives, LANES), F32), exchange2],
        "ssvvvvvvv",
        "vvv",
        [acc, pltpu.VMEM(param[0], F32)],
        name="middle",
    )(tab, lst, own, inc, grad, diag, direction, sent, got)
    got2 = lax.all_to_all(sent2, "drive", split_axis=0, concat_axis=0, tiled=True)
    resid, precond, steps, sent3 = call(
        dots_kernel,
        [param, param, ((SUB, LANES), F32), ((lanes, SUB, LANES), F32)],
        "svvvvvvv",
        "vvvv",
        name="dots",
    )(tab, grad, diag, direction, image, values, sent2, got2)
    got3 = lax.all_to_all(sent3, "drive", split_axis=0, concat_axis=0, tiled=True)
    shape = ((drives, NBLK // street_size, PARAMS), F32)
    parts = call(
        last_kernel,
        [shape] * 5,
        "sssvvvvvvvvvvvv",
        "vvvvv",
        [acc, pltpu.VMEM(param[0], F32)],
        name="last",
        cost_estimate=pl.CostEstimate(flops=200000000, bytes_accessed=8000000, transcendentals=0),
    )(meta, tab, lst, own, inc, direction, image, values, sent, got, sent2, got2, resid, precond, steps)
    return tuple(
        call(finish_kernel, [shape, shape], "vvvvvvv", "vv", name="finish")(steps, got3, *parts)
    )


def solution(mesh):
    placed = (
        P(("region", "drive")),
        P("region", None),
        P("region", None),
        P(("region", "drive"), "street"),
        P(("region", "drive"), "street"),
        P(("region", "drive"), "street"),
        P(None, ("region", "drive"), "street"),
        P(None, ("region", "drive"), "street"),
        P(("region", "drive"), "street"),
        P(("region", "drive"), "street"),
    )
    return jax.shard_map(
        body,
        mesh=mesh,
        in_specs=placed,
        out_specs=(P(("region", "drive"), "street", None), P(("region", "drive"), "street", None)),
        check_vma=False,
    )
```

```python
import jax
import jax.numpy as jnp
from jax import lax
from jax.experimental import pallas as pl
from jax.experimental.pallas import tpu as pltpu
from jax.sharding import PartitionSpec as P

NBLK = 8
DOF = 6
PARAMS = 384
MATCH = 4
LANES = 128
HIGH = 4
CAP = 2
SUB = 8
UNROLL = 13
F32 = jnp.float32
BF16 = jnp.bfloat16


def iota(shape, dim):
    return lax.broadcasted_iota(jnp.int32, shape, dim)


def take_lanes(values, index):
    return jnp.take_along_axis(values, index, axis=1, mode="promise_in_bounds")


def row_of(block, row, count=SUB):
    return jnp.broadcast_to(block[row : row + 1, :], (count, LANES))


def basis_of(s):
    remain = 1.0 - s
    square = s * s
    cube = square * s
    return (
        remain * remain * remain * (1.0 / 6.0),
        (3.0 * cube - 6.0 * square + 4.0) * (1.0 / 6.0),
        (-3.0 * cube + 3.0 * square + 3.0 * s + 1.0) * (1.0 / 6.0),
        cube * (1.0 / 6.0),
    )


def split_two(values):
    high = values.astype(BF16)
    low = (values - high.astype(F32)).astype(BF16)
    return jnp.concatenate([high, low], axis=1)


def places():
    return iota((LANES, LANES), 0).astype(F32).astype(BF16)


def spread(place, knot, kinds):
    low = jnp.bitwise_and(knot, LANES - 1).astype(F32)
    high = jnp.right_shift(knot, 7)
    low = jnp.concatenate([low, low], axis=0).astype(BF16)
    low = jnp.concatenate([low] * (LANES // 16), axis=0)
    hot = jnp.where(place == low, jnp.ones((), BF16), jnp.zeros((), BF16))
    hot = jnp.concatenate([hot, hot], axis=1)
    masks = []
    for h in range(HIGH):
        mask = jnp.where(high == h, 1.0, 0.0)
        mask = jnp.concatenate([mask, mask], axis=0).astype(BF16)
        mask = jnp.concatenate([mask, mask], axis=0)
        masks.append(jnp.concatenate([mask, mask], axis=1))
    sums = []
    for kind in kinds:
        parts = split_two(jnp.concatenate(kind, axis=0))
        left = jnp.concatenate([parts * mask for mask in masks], axis=0)
        sums.append(
            lax.dot_general(left, hot, (((1,), (1,)), ((), ())), preferred_element_type=F32)
        )
    return jnp.concatenate(sums, axis=0)


def fold_shifts(acc, base):
    lane = iota((SUB, LANES), 1)
    out = []
    before = None
    for h in range(HIGH):
        tiles = [acc[base + h * 32 + k * SUB : base + h * 32 + (k + 1) * SUB, :] for k in range(4)]
        rolled = [None] + [pltpu.roll(tiles[k], k, axis=1) for k in range(1, 4)]
        total = tiles[0]
        for k in range(1, 4):
            other = before[k] if before is not None else jnp.zeros((SUB, LANES), F32)
            total = total + jnp.where(lane >= k, rolled[k], other)
        out.append(total)
        before = rolled
    return out


def gather_value(tiles, knot, basis, normals):
    total = None
    for k in range(4):
        index = knot + k
        low = jnp.bitwise_and(index, LANES - 1)
        high = jnp.right_shift(index, 7)
        value = take_lanes(tiles[HIGH - 1], low)
        for h in range(HIGH - 1):
            value = jnp.where(high == h, take_lanes(tiles[h], low), value)
        term = basis[k] * value
        total = term if total is None else total + term
    return jnp.sum(normals * total, axis=0, keepdims=True)


def own_tile(own_ref, h, a):
    normals = own_ref[h, a, 0:SUB, :]
    info = own_ref[h, a, SUB : 2 * SUB, :]
    return normals, row_of(info, 0).astype(jnp.int32), basis_of(row_of(info, 1)), row_of(info, 2)


def inc_tile(inc_ref, block, rank):
    tile = jnp.concatenate([inc_ref[block, 2 * rank], inc_ref[block, 2 * rank + 1]], axis=0)
    info = inc_ref[block, 4]
    knot = jnp.where(rank == 0, info[0:1], info[1:2])
    normals = jnp.where(iota((SUB, LANES), 0) < DOF, tile, 0.0)
    knot = jnp.broadcast_to(knot, (SUB, LANES)).astype(jnp.int32)
    return normals, knot, basis_of(row_of(tile, 6)), row_of(tile, 7)


def decode(code, street_size):
    pick = jnp.bitwise_and(code, 3)
    tile = jnp.right_shift(code, 2)
    rank = jnp.bitwise_and(tile, 1)
    block = jnp.right_shift(tile, 1)
    shift = street_size.bit_length() - 1
    assert street_size == 1 << shift
    lane = jnp.right_shift(block, shift)
    part = jnp.bitwise_and(block, street_size - 1)
    return pick, rank, block, lane, part


def send_kernel(
    meta, counts, dev, picks, knot_own, knot_par, match, spline, geometry, weight, resid,
    send, own, tab, filled, taken, normals_s, knots_s, match_s,
):
    drives = counts.shape[0]
    lanes = send.shape[0]
    street_size = send.shape[1]
    lane = meta[0]
    street = meta[1]
    for j in range(lanes):
        taken[j] = 0
        filled[2 * j] = -1
        filled[2 * j + 1] = -1
    for a in range(drives):
        for m in range(MATCH):
            e = a * MATCH + m
            dest = dev[m, lane * drives + a]
            rank = taken[dest]
            taken[dest] = rank + 1
            tab[e] = dest
            tab[drives * MATCH + e] = rank
            filled[2 * dest + rank] = e
    slot = street * LANES + iota((1, LANES), 1)
    zero1 = jnp.zeros((1, LANES), F32)
    for a in range(drives):
        w = jnp.where(slot < counts[a], weight[a : a + 1, :], 0.0)
        root = jnp.sqrt(w)
        rho = -(root * resid[a : a + 1, :])
        own[a, 0:SUB, :] = jnp.concatenate(
            [geometry[d, a : a + 1, :] * root for d in range(DOF)] + [zero1] * 2, axis=0
        )
        own[a, SUB : 2 * SUB, :] = jnp.concatenate(
            [knot_own[a : a + 1, :].astype(F32), spline[0, a : a + 1, :], rho] + [zero1] * 5, axis=0
        )
        normals_s[a] = jnp.concatenate(
            [-(geometry[DOF + d, a : a + 1, :] * root) for d in range(DOF)]
            + [spline[1, a : a + 1, :], rho],
            axis=0,
        )
        knots_s[a] = jnp.broadcast_to(knot_par[a : a + 1, :].astype(F32), (4, LANES))
        match_s[a] = jnp.broadcast_to(match[a : a + 1, :], (SUB, LANES))
    row = iota((4, LANES), 0)
    for j in range(lanes):
        normals = []
        infos = []
        flags = []
        for r in range(CAP):
            e = filled[2 * j + r]
            safe = jnp.maximum(e, 0)
            a = jnp.right_shift(safe, 2)
            m = jnp.where(e < 0, -1, jnp.bitwise_and(safe, 3))
            pick = picks[jnp.bitwise_and(safe, 3), lane * drives + a]
            there = jnp.logical_and(e >= 0, counts[a] > street * LANES)
            flags.append(jnp.where(there, pick + 1, 0).astype(F32))
            normals.append(jnp.where(match_s[a] == m, normals_s[a], 0.0))
            infos.append(knots_s[a])
        info = jnp.where(row == 0, infos[0], infos[1])
        info = jnp.where(row == 2, flags[0], jnp.where(row == 3, flags[1], info))
        for t in range(street_size):
            for r in range(CAP):
                send[j, t, 2 * r] = normals[r][0:4]
                send[j, t, 2 * r + 1] = normals[r][4:8]
            send[j, t, 4] = info


def put_values(out_ref, tab, own_ref, inc_ref, lst, tiles_ref):
    street_size, drives = own_ref.shape[0], own_ref.shape[1]
    entries = drives * MATCH
    for a in range(drives):
        tiles = [tiles_ref[a, h] for h in range(HIGH)]
        for s in range(street_size):
            normals, knot, basis, _ = own_tile(own_ref, s, a)
            value = gather_value(tiles, knot, basis, normals)
            for m in range(MATCH):
                e = a * MATCH + m
                out_ref[tab[e], tab[entries + e] * street_size + s] = value

    def one(code):
        pick, rank, block, lane, part = decode(code, street_size)
        normals, knot, basis, _ = inc_tile(inc_ref, block, rank)
        value = gather_value([tiles_ref[pick, h] for h in range(HIGH)], knot, basis, normals)
        out_ref[lane, (CAP + rank) * street_size + part] = value

    count = lst[lst.shape[0] - 1]

    def some(i, carry):
        for j in range(UNROLL):
            one(lst[UNROLL * i + j])
        return carry

    lax.fori_loop(0, lax.div(count + UNROLL - 1, UNROLL), some, 0)


def own_sum(sent, got, tab, a, s, street_size, entries):
    e = a * MATCH
    total = sent[tab[e], tab[entries + e] * street_size + s]
    for m in range(MATCH):
        e = a * MATCH + m
        total = total + got[tab[e], (CAP + tab[entries + e]) * street_size + s]
    return total


def inc_sum(sent, got, rank, lane, part, street_size):
    return (
        got[lane, rank * street_size + part]
        + sent[lane, (CAP + rank) * street_size + part]
    )


def spread_own(acc, own_ref, kinds_own):
    street_size, drives = own_ref.shape[0], own_ref.shape[1]
    place = places()
    for a in range(drives):
        total = None
        for s in range(street_size):
            normals, knot, basis, rho = own_tile(own_ref, s, a)
            coeffs = [basis[k] * normals for k in range(4)]
            part = spread(place, knot, kinds_own(coeffs, rho, a, s))
            total = part if total is None else total + part
        acc[a] = total


def spread_inc(acc, street_size, inc_ref, lst, kinds_inc):
    place = places()
    count = lst[lst.shape[0] - 1]

    def one(index):
        pick, rank, block, lane, part = decode(lst[index], street_size)
        normals, knot, basis, rho = inc_tile(inc_ref, block, rank)
        normals = jnp.where(index < count, normals, 0.0)
        coeffs = [basis[k] * normals for k in range(4)]
        return pick, spread(place, knot, kinds_inc(coeffs, rho, rank, lane, part))

    def some(i, carry):
        for pick, value in [one(UNROLL * i + j) for j in range(UNROLL)]:
            acc[pick] = acc[pick] + value
        return carry

    lax.fori_loop(0, lax.div(count + UNROLL - 1, UNROLL), some, 0)


def start_kinds(coeffs, rho, *_):
    return [[c * rho for c in coeffs], [c * c for c in coeffs]]


def own_kernel(own, acc):
    spread_own(acc, own, start_kinds)


def start_kernel(tab, own, inc, begun, grad, diag, direction, out, lst, acc):
    drives = own.shape[1]
    street_size = own.shape[0]
    blocks = inc.shape[0]
    count = 0
    for first in range(0, blocks, 4):
        digits = inc[first, 4]
        for i in range(1, 4):
            digits = digits + inc[first + i, 4] * float(8**i)
        digits = (digits[2:3] + digits[3:4] * float(8**4)).astype(jnp.int32)[0, 0]
        for i in range(4):
            for r in range(CAP):
                flag = jnp.bitwise_and(jnp.right_shift(digits, 3 * (4 * r + i)), 7)
                lst[count] = ((first + i) * CAP + r) * 4 + flag - 1
                count = count + jnp.where(flag > 0, 1, 0)
    last = lst[jnp.maximum(count - 1, 0)]
    for i in range(UNROLL - 1):
        lst[count + i] = last
    lst[lst.shape[0] - 1] = count

    acc[...] = begun[...]
    spread_inc(acc, street_size, inc, lst, start_kinds)
    for a in range(drives):
        sums = acc[a]
        gradient = fold_shifts(sums, 0)
        squares = fold_shifts(sums, 128)
        for h in range(HIGH):
            diagonal = 1.0 + squares[h]
            grad[a, h] = gradient[h]
            diag[a, h] = diagonal
            direction[a, h] = gradient[h] / diagonal
    out[...] = jnp.zeros(out.shape, F32)
    put_values(out, tab, own, inc, lst, direction)


def scalar_row(values):
    lane = iota((1, LANES), 1)
    row = jnp.zeros((1, LANES), F32)
    for i, value in enumerate(values):
        total = jnp.sum(jnp.sum(value, axis=0, keepdims=True), axis=1, keepdims=True)
        row = jnp.where(lane == i, total, row)
    return row


def pick_lane(row, i):
    return jnp.sum(jnp.where(iota((1, LANES), 1) == i, row, 0.0), axis=1, keepdims=True)


def middle_kernel(
    tab, lst, own, inc, grad, diag, direction, sent, got, image, values, out, acc, ratio
):
    street_size, drives = own.shape[0], own.shape[1]
    entries = drives * MATCH
    for a in range(drives):
        for s in range(street_size):
            values[pl.ds(s * drives + a, 1), :] = own_sum(sent, got, tab, a, s, street_size, entries)

    def kinds_own(coeffs, rho, a, s):
        value = jnp.broadcast_to(values[pl.ds(s * drives + a, 1), :], (SUB, LANES))
        return [[c * value for c in coeffs]]

    def kinds_inc(coeffs, rho, rank, lane, part):
        value = inc_sum(sent, got, rank, lane, part, street_size)
        value = jnp.broadcast_to(value, (SUB, LANES))
        return [[c * value for c in coeffs]]

    spread_own(acc, own, kinds_own)
    spread_inc(acc, street_size, inc, lst, kinds_inc)
    first = jnp.zeros((SUB, LANES), F32)
    second = jnp.zeros((SUB, LANES), F32)
    for a in range(drives):
        sums = fold_shifts(acc[a], 0)
        for h in range(HIGH):
            p = direction[a, h]
            q = p + sums[h]
            image[a, h] = q
            ratio[a, h] = q / diag[a, h]
            first = first + grad[a, h] * p
            second = second + p * q
    out[...] = jnp.zeros(out.shape, F32)
    put_values(out, tab, own, inc, lst, ratio)
    row = scalar_row([first, second])
    rows = 2 * CAP * street_size
    for j in range(out.shape[0]):
        out[j, rows] = row


def dots_kernel(tab, grad, diag, direction, image, values, sent, got, resid, precond, steps, out):
    drives = grad.shape[0]
    street_size = values.shape[0] // drives
    entries = drives * MATCH
    rows = 2 * CAP * street_size
    total = got[0, rows]
    for j in range(1, got.shape[0]):
        total = total + got[j, rows]
    inner = pick_lane(total, 0)
    curve = pick_lane(total, 1)
    alpha = inner / curve
    one = jnp.zeros((SUB, LANES), F32)
    two = jnp.zeros((SUB, LANES), F32)
    three = jnp.zeros((SUB, LANES), F32)
    for a in range(drives):
        for h in range(HIGH):
            r = grad[a, h] - alpha * image[a, h]
            z = r / diag[a, h]
            resid[a, h] = r
            precond[a, h] = z
            one = one + r * z
            two = two + z * z
            three = three + z * direction[a, h]
    slots2 = jnp.zeros((1, LANES), F32)
    slots3 = jnp.zeros((1, LANES), F32)
    for a in range(drives):
        for s in range(street_size):
            before = values[pl.ds(s * drives + a, 1), :]
            value = before - alpha * own_sum(sent, got, tab, a, s, street_size, entries)
            slots2 = slots2 + value * value
            slots3 = slots3 + value * before
    head = iota((SUB, LANES), 0) == 0
    two = two + jnp.where(head, jnp.broadcast_to(slots2, (SUB, LANES)), 0.0)
    three = three + jnp.where(head, jnp.broadcast_to(slots3, (SUB, LANES)), 0.0)
    row = scalar_row([one, two, three])
    for j in range(out.shape[0]):
        out[j] = row
    lane = iota((SUB, LANES), 1)
    steps[...] = jnp.where(lane == 0, alpha, jnp.where(lane == 1, inner, curve))


def last_kernel(
    meta, tab, lst, own, inc, direction, image, values, sent, got, sent2, got2, resid, precond,
    steps, o_p, o_z, o_r, o_h, o_q, acc, hess,
):
    street_size, drives = own.shape[0], own.shape[1]
    entries = drives * MATCH
    alpha = steps[0:1, 0:1]

    def kinds_own(coeffs, rho, a, s):
        value = values[pl.ds(s * drives + a, 1), :] - alpha * own_sum(
            sent2, got2, tab, a, s, street_size, entries
        )
        value = jnp.broadcast_to(value, (SUB, LANES))
        return [[c * value for c in coeffs]]

    def kinds_inc(coeffs, rho, rank, lane, part):
        value = inc_sum(sent, got, rank, lane, part, street_size) - alpha * inc_sum(
            sent2, got2, rank, lane, part, street_size
        )
        value = jnp.broadcast_to(value, (SUB, LANES))
        return [[c * value for c in coeffs]]

    spread_own(acc, own, kinds_own)
    spread_inc(acc, street_size, inc, lst, kinds_inc)
    for a in range(drives):
        sums = fold_shifts(acc[a], 0)
        for h in range(HIGH):
            hess[a, h] = precond[a, h] + sums[h]
    blocks = o_p.shape[1]
    tiles = PARAMS // LANES
    row = iota((SUB, LANES), 0)
    points = []
    masks = []
    for q in range(tiles):
        entry = q * LANES + iota((SUB, LANES), 1)
        point = jnp.right_shift(entry * 10923, 16)
        points.append(point)
        masks.append(row == entry - point * DOF)
    for bl in range(blocks):
        block = meta[1] * blocks + bl
        high = jnp.right_shift(block, 1)
        offset = jnp.bitwise_and(block, 1) * (LANES // 2)
        indices = [offset + points[q] for q in range(tiles)]
        for a in range(drives):
            for source, target in (
                (direction, o_p), (precond, o_z), (resid, o_r), (hess, o_h), (image, o_q)
            ):
                tile = source[a, high]
                for q in range(tiles):
                    value = jnp.where(masks[q], take_lanes(tile, indices[q]), 0.0)
                    target[a, bl : bl + 1, q * LANES : (q + 1) * LANES] = jnp.sum(
                        value, axis=0, keepdims=True
                    )


def finish_kernel(steps, got, o_p, o_z, o_r, o_h, o_q, step_out, resid_out):
    total = got[0]
    for j in range(1, got.shape[0]):
        total = total + got[j]
    inner_next = pick_lane(total, 0)
    alpha = steps[0:1, 0:1]
    inner = steps[0:1, 1:2]
    curve = steps[0:1, 2:3]
    beta = inner_next / inner
    denominator = pick_lane(total, 1) + 2.0 * beta * pick_lane(total, 2) + beta * beta * curve
    last = inner_next / denominator
    for a in range(o_p.shape[0]):
        p = o_p[a]
        step_out[a] = alpha * p + last * (o_z[a] + beta * p)
        resid_out[a] = o_r[a] - last * (o_h[a] + beta * o_q[a])


def call(kernel, shapes, spaces_in, spaces_out, scratch=(), **kwargs):
    where = {"s": pltpu.SMEM, "v": pltpu.VMEM}
    return pl.pallas_call(
        kernel,
        out_shape=[jax.ShapeDtypeStruct(s, d) for s, d in shapes],
        in_specs=[pl.BlockSpec(memory_space=where[c]) for c in spaces_in],
        out_specs=[pl.BlockSpec(memory_space=where[c]) for c in spaces_out],
        scratch_shapes=list(scratch),
        compiler_params=pltpu.CompilerParams(vmem_limit_bytes=40 * 1024 * 1024),
        **kwargs,
    )


def body(
    pt_count,
    partner_dev,
    partner_pick,
    knot_own,
    knot_partner,
    match_slot,
    spline,
    geometry,
    point_weight,
    point_resid,
):
    drives = knot_own.shape[0]
    lanes = lax.axis_size("drive")
    street_size = lax.axis_size("street")
    meta = jnp.stack([lax.axis_index("drive"), lax.axis_index("street")]).astype(jnp.int32)
    entries = drives * MATCH
    blocks = lanes * street_size
    param = ((drives, HIGH, SUB, LANES), F32)
    arrays = (
        pt_count, partner_dev.T, partner_pick.T, knot_own, knot_partner, match_slot,
        spline, geometry, point_weight, point_resid,
    )
    send, mine, tab = call(
        send_kernel,
        [
            ((lanes, street_size, 5, 4, LANES), F32),
            ((drives, 2 * SUB, LANES), F32),
            ((2 * entries,), jnp.int32),
        ],
        "ssssvvvvvvv",
        "vvs",
        [
            pltpu.SMEM((CAP * lanes,), jnp.int32),
            pltpu.SMEM((lanes,), jnp.int32),
            pltpu.VMEM((drives, SUB, LANES), F32),
            pltpu.VMEM((drives, 4, LANES), F32),
            pltpu.VMEM((drives, SUB, LANES), jnp.int32),
        ],
        name="send",
    )(meta, *arrays)
    if street_size == 2:
        peer = lax.ppermute(mine, "street", [(0, 1), (1, 0)])
        first = meta[1] == 0
        own = jnp.stack([jnp.where(first, mine, peer), jnp.where(first, peer, mine)])
    else:
        own = lax.all_gather(mine, "street", axis=0, tiled=False)
    inc = lax.all_to_all(
        send.reshape(blocks, 5, 4, LANES), ("drive", "street"), split_axis=0, concat_axis=0, tiled=True
    )
    exchange = ((lanes, 2 * CAP * street_size, 1, LANES), F32)
    exchange2 = ((lanes, 2 * CAP * street_size + 1, 1, LANES), F32)
    acc = pltpu.VMEM((drives, 128, LANES), F32)
    list_size = CAP * blocks + UNROLL
    (begun,) = call(
        own_kernel,
        [((drives, 256, LANES), F32)],
        "v",
        "v",
        name="own",
        cost_estimate=pl.CostEstimate(flops=70000000, bytes_accessed=1000000, transcendentals=0),
    )(own)
    grad, diag, direction, sent, lst = call(
        start_kernel,
        [param, param, param, exchange, ((list_size,), jnp.int32)],
        "svvv",
        "vvvvs",
        [pltpu.VMEM((drives, 256, LANES), F32)],
        name="start",
    )(tab, own, inc, begun)
    got = lax.all_to_all(sent, "drive", split_axis=0, concat_axis=0, tiled=True)
    image, values, sent2 = call(
        middle_kernel,
        [param, ((street_size * drives, LANES), F32), exchange2],
        "ssvvvvvvv",
        "vvv",
        [acc, pltpu.VMEM(param[0], F32)],
        name="middle",
    )(tab, lst, own, inc, grad, diag, direction, sent, got)
    got2 = lax.all_to_all(sent2, "drive", split_axis=0, concat_axis=0, tiled=True)
    resid, precond, steps, sent3 = call(
        dots_kernel,
        [param, param, ((SUB, LANES), F32), ((lanes, 1, LANES), F32)],
        "svvvvvvv",
        "vvvv",
        name="dots",
    )(tab, grad, diag, direction, image, values, sent2, got2)
    got3 = lax.all_to_all(sent3, "drive", split_axis=0, concat_axis=0, tiled=True)
    shape = ((drives, NBLK // street_size, PARAMS), F32)
    parts = call(
        last_kernel,
        [shape] * 5,
        "sssvvvvvvvvvvvv",
        "vvvvv",
        [acc, pltpu.VMEM(param[0], F32)],
        name="last",
        cost_estimate=pl.CostEstimate(flops=200000000, bytes_accessed=8000000, transcendentals=0),
    )(meta, tab, lst, own, inc, direction, image, values, sent, got, sent2, got2, resid, precond, steps)
    return tuple(
        call(finish_kernel, [shape, shape], "vvvvvvv", "vv", name="finish")(steps, got3, *parts)
    )


def solution(mesh):
    placed = (
        P(("region", "drive")),
        P("region", None),
        P("region", None),
        P(("region", "drive"), "street"),
        P(("region", "drive"), "street"),
        P(("region", "drive"), "street"),
        P(None, ("region", "drive"), "street"),
        P(None, ("region", "drive"), "street"),
        P(("region", "drive"), "street"),
        P(("region", "drive"), "street"),
    )
    return jax.shard_map(
        body,
        mesh=mesh,
        in_specs=placed,
        out_specs=(P(("region", "drive"), "street", None), P(("region", "drive"), "street", None)),
        check_vma=False,
    )
```

```python
import jax
import jax.numpy as jnp
from jax import lax
from jax.experimental import pallas as pl
from jax.experimental.pallas import tpu as pltpu
from jax.sharding import PartitionSpec as P

NBLK = 8
DOF = 6
PARAMS = 384
MATCH = 4
LANES = 128
HIGH = 4
CAP = 2
SUB = 8
UNROLL = 13
F32 = jnp.float32
BF16 = jnp.bfloat16


def iota(shape, dim):
    return lax.broadcasted_iota(jnp.int32, shape, dim)


def take_lanes(values, index):
    return jnp.take_along_axis(values, index, axis=1, mode="promise_in_bounds")


def row_of(block, row, count=SUB):
    return jnp.broadcast_to(block[row : row + 1, :], (count, LANES))


def basis_of(s):
    remain = 1.0 - s
    square = s * s
    cube = square * s
    return (
        remain * remain * remain * (1.0 / 6.0),
        (3.0 * cube - 6.0 * square + 4.0) * (1.0 / 6.0),
        (-3.0 * cube + 3.0 * square + 3.0 * s + 1.0) * (1.0 / 6.0),
        cube * (1.0 / 6.0),
    )


def split_two(values):
    high = values.astype(BF16)
    low = (values - high.astype(F32)).astype(BF16)
    return jnp.concatenate([high, low], axis=1)


def places():
    return iota((LANES, LANES), 0).astype(F32).astype(BF16)


def spread(place, knot, kinds):
    low = jnp.bitwise_and(knot, LANES - 1).astype(F32)
    high = jnp.right_shift(knot, 7)
    low = jnp.concatenate([low, low], axis=0).astype(BF16)
    low = jnp.concatenate([low] * (LANES // 16), axis=0)
    hot = jnp.where(place == low, jnp.ones((), BF16), jnp.zeros((), BF16))
    hot = jnp.concatenate([hot, hot], axis=1)
    masks = []
    for h in range(HIGH):
        mask = jnp.where(high == h, 1.0, 0.0)
        mask = jnp.concatenate([mask, mask], axis=0).astype(BF16)
        mask = jnp.concatenate([mask, mask], axis=0)
        masks.append(jnp.concatenate([mask, mask], axis=1))
    sums = []
    for kind in kinds:
        parts = split_two(jnp.concatenate(kind, axis=0))
        left = jnp.concatenate([parts * mask for mask in masks], axis=0)
        sums.append(
            lax.dot_general(left, hot, (((1,), (1,)), ((), ())), preferred_element_type=F32)
        )
    return jnp.concatenate(sums, axis=0)


def fold_shifts(acc, base):
    lane = iota((SUB, LANES), 1)
    out = []
    before = None
    for h in range(HIGH):
        tiles = [acc[base + h * 32 + k * SUB : base + h * 32 + (k + 1) * SUB, :] for k in range(4)]
        rolled = [None] + [pltpu.roll(tiles[k], k, axis=1) for k in range(1, 4)]
        total = tiles[0]
        for k in range(1, 4):
            other = before[k] if before is not None else jnp.zeros((SUB, LANES), F32)
            total = total + jnp.where(lane >= k, rolled[k], other)
        out.append(total)
        before = rolled
    return out


def gather_value(tiles, knot, basis, normals):
    total = None
    for k in range(4):
        index = knot + k
        low = jnp.bitwise_and(index, LANES - 1)
        high = jnp.right_shift(index, 7)
        value = take_lanes(tiles[HIGH - 1], low)
        for h in range(HIGH - 1):
            value = jnp.where(high == h, take_lanes(tiles[h], low), value)
        term = basis[k] * value
        total = term if total is None else total + term
    return jnp.sum(normals * total, axis=0, keepdims=True)


def own_tile(own_ref, h, a):
    normals = own_ref[h, a, 0:SUB, :]
    info = own_ref[h, a, SUB : 2 * SUB, :]
    return normals, row_of(info, 0).astype(jnp.int32), basis_of(row_of(info, 1)), row_of(info, 2)


def inc_tile(inc_ref, block, rank):
    tile = jnp.concatenate([inc_ref[block, 2 * rank], inc_ref[block, 2 * rank + 1]], axis=0)
    info = inc_ref[block, 4]
    knot = jnp.where(rank == 0, info[0:1], info[1:2])
    normals = jnp.where(iota((SUB, LANES), 0) < DOF, tile, 0.0)
    knot = jnp.broadcast_to(knot, (SUB, LANES)).astype(jnp.int32)
    return normals, knot, basis_of(row_of(tile, 6)), row_of(tile, 7)


def decode(code, street_size):
    pick = jnp.bitwise_and(code, 3)
    tile = jnp.right_shift(code, 2)
    rank = jnp.bitwise_and(tile, 1)
    block = jnp.right_shift(tile, 1)
    shift = street_size.bit_length() - 1
    assert street_size == 1 << shift
    lane = jnp.right_shift(block, shift)
    part = jnp.bitwise_and(block, street_size - 1)
    return pick, rank, block, lane, part


def send_kernel(
    counts, dev, picks, knot_own, knot_par, match, spline, geometry, weight, resid,
    send, own, tab, filled, taken, normals_s, knots_s, match_s,
):
    drives = counts.shape[0]
    lanes = send.shape[0]
    street_size = send.shape[1]
    lane = lax.axis_index("drive")
    street = lax.axis_index("street")
    tab[2 * drives * MATCH] = street
    for j in range(lanes):
        taken[j] = 0
        filled[2 * j] = -1
        filled[2 * j + 1] = -1
    for a in range(drives):
        for m in range(MATCH):
            e = a * MATCH + m
            dest = dev[m, lane * drives + a]
            rank = taken[dest]
            taken[dest] = rank + 1
            tab[e] = dest
            tab[drives * MATCH + e] = rank
            filled[2 * dest + rank] = e
    slot = street * LANES + iota((1, LANES), 1)
    zero1 = jnp.zeros((1, LANES), F32)
    for a in range(drives):
        w = jnp.where(slot < counts[a], weight[a : a + 1, :], 0.0)
        root = jnp.sqrt(w)
        rho = -(root * resid[a : a + 1, :])
        own[a, 0:SUB, :] = jnp.concatenate(
            [geometry[d, a : a + 1, :] * root for d in range(DOF)] + [zero1] * 2, axis=0
        )
        own[a, SUB : 2 * SUB, :] = jnp.concatenate(
            [knot_own[a : a + 1, :].astype(F32), spline[0, a : a + 1, :], rho] + [zero1] * 5, axis=0
        )
        normals_s[a] = jnp.concatenate(
            [-(geometry[DOF + d, a : a + 1, :] * root) for d in range(DOF)]
            + [spline[1, a : a + 1, :], rho],
            axis=0,
        )
        knots_s[a] = jnp.broadcast_to(knot_par[a : a + 1, :].astype(F32), (4, LANES))
        match_s[a] = jnp.broadcast_to(match[a : a + 1, :], (SUB, LANES))
    row = iota((4, LANES), 0)
    for j in range(lanes):
        normals = []
        infos = []
        flags = []
        for r in range(CAP):
            e = filled[2 * j + r]
            safe = jnp.maximum(e, 0)
            a = jnp.right_shift(safe, 2)
            m = jnp.where(e < 0, -1, jnp.bitwise_and(safe, 3))
            pick = picks[jnp.bitwise_and(safe, 3), lane * drives + a]
            there = jnp.logical_and(e >= 0, counts[a] > street * LANES)
            flags.append(jnp.where(there, pick + 1, 0).astype(F32))
            normals.append(jnp.where(match_s[a] == m, normals_s[a], 0.0))
            infos.append(knots_s[a])
        info = jnp.where(row == 0, infos[0], infos[1])
        info = jnp.where(row == 2, flags[0], jnp.where(row == 3, flags[1], info))
        for t in range(street_size):
            for r in range(CAP):
                send[j, t, 2 * r] = normals[r][0:4]
                send[j, t, 2 * r + 1] = normals[r][4:8]
            send[j, t, 4] = info


def put_values(out_ref, tab, own_ref, inc_ref, lst, tiles_ref):
    street_size, drives = own_ref.shape[0], own_ref.shape[1]
    entries = drives * MATCH
    for a in range(drives):
        tiles = [tiles_ref[a, h] for h in range(HIGH)]
        for s in range(street_size):
            normals, knot, basis, _ = own_tile(own_ref, s, a)
            value = gather_value(tiles, knot, basis, normals)
            for m in range(MATCH):
                e = a * MATCH + m
                out_ref[tab[e], tab[entries + e] * street_size + s] = value

    def one(code):
        pick, rank, block, lane, part = decode(code, street_size)
        normals, knot, basis, _ = inc_tile(inc_ref, block, rank)
        value = gather_value([tiles_ref[pick, h] for h in range(HIGH)], knot, basis, normals)
        out_ref[lane, (CAP + rank) * street_size + part] = value

    count = lst[lst.shape[0] - 1]

    def some(i, carry):
        for j in range(UNROLL):
            one(lst[UNROLL * i + j])
        return carry

    lax.fori_loop(0, lax.div(count + UNROLL - 1, UNROLL), some, 0)


def own_sum(sent, got, tab, a, s, street_size, entries):
    e = a * MATCH
    total = sent[tab[e], tab[entries + e] * street_size + s]
    for m in range(MATCH):
        e = a * MATCH + m
        total = total + got[tab[e], (CAP + tab[entries + e]) * street_size + s]
    return total


def inc_sum(sent, got, rank, lane, part, street_size):
    return (
        got[lane, rank * street_size + part]
        + sent[lane, (CAP + rank) * street_size + part]
    )


def spread_own(acc, own_ref, kinds_own):
    street_size, drives = own_ref.shape[0], own_ref.shape[1]
    place = places()
    for a in range(drives):
        total = None
        for s in range(street_size):
            normals, knot, basis, rho = own_tile(own_ref, s, a)
            coeffs = [basis[k] * normals for k in range(4)]
            part = spread(place, knot, kinds_own(coeffs, rho, a, s))
            total = part if total is None else total + part
        acc[a] = total


def spread_inc(acc, street_size, inc_ref, lst, kinds_inc):
    place = places()
    count = lst[lst.shape[0] - 1]

    def one(index):
        pick, rank, block, lane, part = decode(lst[index], street_size)
        normals, knot, basis, rho = inc_tile(inc_ref, block, rank)
        normals = jnp.where(index < count, normals, 0.0)
        coeffs = [basis[k] * normals for k in range(4)]
        return pick, spread(place, knot, kinds_inc(coeffs, rho, rank, lane, part))

    def some(i, carry):
        for pick, value in [one(UNROLL * i + j) for j in range(UNROLL)]:
            acc[pick] = acc[pick] + value
        return carry

    lax.fori_loop(0, lax.div(count + UNROLL - 1, UNROLL), some, 0)


def start_kinds(coeffs, rho, *_):
    return [[c * rho for c in coeffs], [c * c for c in coeffs]]


def own_kernel(own, acc):
    spread_own(acc, own, start_kinds)


def start_kernel(tab, own, inc, begun, grad, diag, direction, out, lst, acc):
    drives = own.shape[1]
    street_size = own.shape[0]
    blocks = inc.shape[0]
    count = 0
    for first in range(0, blocks, 4):
        digits = inc[first, 4]
        for i in range(1, 4):
            digits = digits + inc[first + i, 4] * float(8**i)
        digits = (digits[2:3] + digits[3:4] * float(8**4)).astype(jnp.int32)[0, 0]
        for i in range(4):
            for r in range(CAP):
                flag = jnp.bitwise_and(jnp.right_shift(digits, 3 * (4 * r + i)), 7)
                lst[count] = ((first + i) * CAP + r) * 4 + flag - 1
                count = count + jnp.where(flag > 0, 1, 0)
    last = lst[jnp.maximum(count - 1, 0)]
    for i in range(UNROLL - 1):
        lst[count + i] = last
    lst[lst.shape[0] - 1] = count

    acc[...] = begun[...]
    spread_inc(acc, street_size, inc, lst, start_kinds)
    for a in range(drives):
        sums = acc[a]
        gradient = fold_shifts(sums, 0)
        squares = fold_shifts(sums, 128)
        for h in range(HIGH):
            diagonal = 1.0 + squares[h]
            grad[a, h] = gradient[h]
            diag[a, h] = diagonal
            direction[a, h] = gradient[h] / diagonal
    out[...] = jnp.zeros(out.shape, F32)
    put_values(out, tab, own, inc, lst, direction)


def scalar_row(values):
    lane = iota((1, LANES), 1)
    row = jnp.zeros((1, LANES), F32)
    for i, value in enumerate(values):
        total = jnp.sum(jnp.sum(value, axis=0, keepdims=True), axis=1, keepdims=True)
        row = jnp.where(lane == i, total, row)
    return row


def pick_lane(row, i):
    return jnp.sum(jnp.where(iota((1, LANES), 1) == i, row, 0.0), axis=1, keepdims=True)


def middle_kernel(
    tab, lst, own, inc, grad, diag, direction, sent, got, image, values, out, acc, ratio
):
    street_size, drives = own.shape[0], own.shape[1]
    entries = drives * MATCH
    for a in range(drives):
        for s in range(street_size):
            values[pl.ds(s * drives + a, 1), :] = own_sum(sent, got, tab, a, s, street_size, entries)

    def kinds_own(coeffs, rho, a, s):
        value = jnp.broadcast_to(values[pl.ds(s * drives + a, 1), :], (SUB, LANES))
        return [[c * value for c in coeffs]]

    def kinds_inc(coeffs, rho, rank, lane, part):
        value = inc_sum(sent, got, rank, lane, part, street_size)
        value = jnp.broadcast_to(value, (SUB, LANES))
        return [[c * value for c in coeffs]]

    spread_own(acc, own, kinds_own)
    spread_inc(acc, street_size, inc, lst, kinds_inc)
    first = jnp.zeros((SUB, LANES), F32)
    second = jnp.zeros((SUB, LANES), F32)
    for a in range(drives):
        sums = fold_shifts(acc[a], 0)
        for h in range(HIGH):
            p = direction[a, h]
            q = p + sums[h]
            image[a, h] = q
            ratio[a, h] = q / diag[a, h]
            first = first + grad[a, h] * p
            second = second + p * q
    out[...] = jnp.zeros(out.shape, F32)
    put_values(out, tab, own, inc, lst, ratio)
    row = scalar_row([first, second])
    rows = 2 * CAP * street_size
    for j in range(out.shape[0]):
        out[j, rows] = row


def dots_kernel(tab, grad, diag, direction, image, values, sent, got, resid, precond, steps, out):
    drives = grad.shape[0]
    street_size = values.shape[0] // drives
    entries = drives * MATCH
    rows = 2 * CAP * street_size
    total = got[0, rows]
    for j in range(1, got.shape[0]):
        total = total + got[j, rows]
    inner = pick_lane(total, 0)
    curve = pick_lane(total, 1)
    alpha = inner / curve
    one = jnp.zeros((SUB, LANES), F32)
    two = jnp.zeros((SUB, LANES), F32)
    three = jnp.zeros((SUB, LANES), F32)
    for a in range(drives):
        for h in range(HIGH):
            r = grad[a, h] - alpha * image[a, h]
            z = r / diag[a, h]
            resid[a, h] = r
            precond[a, h] = z
            one = one + r * z
            two = two + z * z
            three = three + z * direction[a, h]
    slots2 = jnp.zeros((1, LANES), F32)
    slots3 = jnp.zeros((1, LANES), F32)
    for a in range(drives):
        for s in range(street_size):
            before = values[pl.ds(s * drives + a, 1), :]
            value = before - alpha * own_sum(sent, got, tab, a, s, street_size, entries)
            slots2 = slots2 + value * value
            slots3 = slots3 + value * before
    head = iota((SUB, LANES), 0) == 0
    two = two + jnp.where(head, jnp.broadcast_to(slots2, (SUB, LANES)), 0.0)
    three = three + jnp.where(head, jnp.broadcast_to(slots3, (SUB, LANES)), 0.0)
    row = scalar_row([one, two, three])
    for j in range(out.shape[0]):
        out[j] = row
    lane = iota((SUB, LANES), 1)
    steps[...] = jnp.where(lane == 0, alpha, jnp.where(lane == 1, inner, curve))


def last_kernel(
    tab, lst, own, inc, direction, image, values, sent, got, sent2, got2, resid, precond,
    steps, o_p, o_z, o_r, o_h, o_q, acc, hess,
):
    street_size, drives = own.shape[0], own.shape[1]
    entries = drives * MATCH
    alpha = steps[0:1, 0:1]

    def kinds_own(coeffs, rho, a, s):
        value = values[pl.ds(s * drives + a, 1), :] - alpha * own_sum(
            sent2, got2, tab, a, s, street_size, entries
        )
        value = jnp.broadcast_to(value, (SUB, LANES))
        return [[c * value for c in coeffs]]

    def kinds_inc(coeffs, rho, rank, lane, part):
        value = inc_sum(sent, got, rank, lane, part, street_size) - alpha * inc_sum(
            sent2, got2, rank, lane, part, street_size
        )
        value = jnp.broadcast_to(value, (SUB, LANES))
        return [[c * value for c in coeffs]]

    spread_own(acc, own, kinds_own)
    spread_inc(acc, street_size, inc, lst, kinds_inc)
    for a in range(drives):
        sums = fold_shifts(acc[a], 0)
        for h in range(HIGH):
            hess[a, h] = precond[a, h] + sums[h]
    blocks = o_p.shape[1]
    tiles = PARAMS // LANES
    row = iota((SUB, LANES), 0)
    points = []
    masks = []
    for q in range(tiles):
        entry = q * LANES + iota((SUB, LANES), 1)
        point = jnp.right_shift(entry * 10923, 16)
        points.append(point)
        masks.append(row == entry - point * DOF)
    for bl in range(blocks):
        block = tab[2 * entries] * blocks + bl
        high = jnp.right_shift(block, 1)
        offset = jnp.bitwise_and(block, 1) * (LANES // 2)
        indices = [offset + points[q] for q in range(tiles)]
        for a in range(drives):
            for source, target in (
                (direction, o_p), (precond, o_z), (resid, o_r), (hess, o_h), (image, o_q)
            ):
                tile = source[a, high]
                for q in range(tiles):
                    value = jnp.where(masks[q], take_lanes(tile, indices[q]), 0.0)
                    target[a, bl : bl + 1, q * LANES : (q + 1) * LANES] = jnp.sum(
                        value, axis=0, keepdims=True
                    )


def finish_kernel(steps, got, o_p, o_z, o_r, o_h, o_q, step_out, resid_out):
    total = got[0]
    for j in range(1, got.shape[0]):
        total = total + got[j]
    inner_next = pick_lane(total, 0)
    alpha = steps[0:1, 0:1]
    inner = steps[0:1, 1:2]
    curve = steps[0:1, 2:3]
    beta = inner_next / inner
    denominator = pick_lane(total, 1) + 2.0 * beta * pick_lane(total, 2) + beta * beta * curve
    last = inner_next / denominator
    for a in range(o_p.shape[0]):
        p = o_p[a]
        step_out[a] = alpha * p + last * (o_z[a] + beta * p)
        resid_out[a] = o_r[a] - last * (o_h[a] + beta * o_q[a])


def call(kernel, shapes, spaces_in, spaces_out, scratch=(), limit=40, **kwargs):
    where = {"s": pltpu.SMEM, "v": pltpu.VMEM}
    return pl.pallas_call(
        kernel,
        out_shape=[jax.ShapeDtypeStruct(s, d) for s, d in shapes],
        in_specs=[pl.BlockSpec(memory_space=where[c]) for c in spaces_in],
        out_specs=[pl.BlockSpec(memory_space=where[c]) for c in spaces_out],
        scratch_shapes=list(scratch),
        compiler_params=pltpu.CompilerParams(vmem_limit_bytes=limit * 1024 * 1024),
        **kwargs,
    )


def body(
    pt_count,
    partner_dev,
    partner_pick,
    knot_own,
    knot_partner,
    match_slot,
    spline,
    geometry,
    point_weight,
    point_resid,
):
    drives = knot_own.shape[0]
    lanes = lax.axis_size("drive")
    street_size = lax.axis_size("street")
    entries = drives * MATCH
    blocks = lanes * street_size
    param = ((drives, HIGH, SUB, LANES), F32)
    arrays = (
        pt_count, partner_dev.T, partner_pick.T, knot_own, knot_partner, match_slot,
        spline, geometry, point_weight, point_resid,
    )
    send, mine, tab = call(
        send_kernel,
        [
            ((lanes, street_size, 5, 4, LANES), F32),
            ((drives, 2 * SUB, LANES), F32),
            ((2 * entries + 1,), jnp.int32),
        ],
        "sssvvvvvvv",
        "vvs",
        [
            pltpu.SMEM((CAP * lanes,), jnp.int32),
            pltpu.SMEM((lanes,), jnp.int32),
            pltpu.VMEM((drives, SUB, LANES), F32),
            pltpu.VMEM((drives, 4, LANES), F32),
            pltpu.VMEM((drives, SUB, LANES), jnp.int32),
        ],
        name="send",
        limit=60,
    )(*arrays)
    if street_size == 2:
        peer = lax.ppermute(mine, "street", [(0, 1), (1, 0)])
        first = lax.axis_index("street") == 0
        own = jnp.stack([jnp.where(first, mine, peer), jnp.where(first, peer, mine)])
    else:
        own = lax.all_gather(mine, "street", axis=0, tiled=False)
    inc = lax.all_to_all(
        send.reshape(blocks, 5, 4, LANES), ("drive", "street"), split_axis=0, concat_axis=0, tiled=True
    )
    exchange = ((lanes, 2 * CAP * street_size, 1, LANES), F32)
    exchange2 = ((lanes, 2 * CAP * street_size + 1, 1, LANES), F32)
    acc = pltpu.VMEM((drives, 128, LANES), F32)
    list_size = CAP * blocks + UNROLL
    (begun,) = call(
        own_kernel,
        [((drives, 256, LANES), F32)],
        "v",
        "v",
        name="own",
        cost_estimate=pl.CostEstimate(flops=70000000, bytes_accessed=1000000, transcendentals=0),
    )(own)
    grad, diag, direction, sent, lst = call(
        start_kernel,
        [param, param, param, exchange, ((list_size,), jnp.int32)],
        "svvv",
        "vvvvs",
        [pltpu.VMEM((drives, 256, LANES), F32)],
        name="start",
    )(tab, own, inc, begun)
    got = lax.all_to_all(sent, "drive", split_axis=0, concat_axis=0, tiled=True)
    image, values, sent2 = call(
        middle_kernel,
        [param, ((street_size * drives, LANES), F32), exchange2],
        "ssvvvvvvv",
        "vvv",
        [acc, pltpu.VMEM(param[0], F32)],
        name="middle",
    )(tab, lst, own, inc, grad, diag, direction, sent, got)
    got2 = lax.all_to_all(sent2, "drive", split_axis=0, concat_axis=0, tiled=True)
    resid, precond, steps, sent3 = call(
        dots_kernel,
        [param, param, ((SUB, LANES), F32), ((lanes, 1, LANES), F32)],
        "svvvvvvv",
        "vvvv",
        name="dots",
    )(tab, grad, diag, direction, image, values, sent2, got2)
    got3 = lax.all_to_all(sent3, "drive", split_axis=0, concat_axis=0, tiled=True)
    shape = ((drives, NBLK // street_size, PARAMS), F32)
    parts = call(
        last_kernel,
        [shape] * 5,
        "ssvvvvvvvvvvvv",
        "vvvvv",
        [acc, pltpu.VMEM(param[0], F32)],
        name="last",
        cost_estimate=pl.CostEstimate(flops=200000000, bytes_accessed=8000000, transcendentals=0),
    )(tab, lst, own, inc, direction, image, values, sent, got, sent2, got2, resid, precond, steps)
    return tuple(
        call(finish_kernel, [shape, shape], "vvvvvvv", "vv", name="finish")(steps, got3, *parts)
    )


def solution(mesh):
    placed = (
        P(("region", "drive")),
        P("region", None),
        P("region", None),
        P(("region", "drive"), "street"),
        P(("region", "drive"), "street"),
        P(("region", "drive"), "street"),
        P(None, ("region", "drive"), "street"),
        P(None, ("region", "drive"), "street"),
        P(("region", "drive"), "street"),
        P(("region", "drive"), "street"),
    )
    return jax.shard_map(
        body,
        mesh=mesh,
        in_specs=placed,
        out_specs=(P(("region", "drive"), "street", None), P(("region", "drive"), "street", None)),
        check_vma=False,
    )
```

```python
import jax
import jax.numpy as jnp
from jax import lax
from jax.experimental import pallas as pl
from jax.experimental.pallas import tpu as pltpu
from jax.sharding import PartitionSpec as P

NBLK = 8
DOF = 6
PARAMS = 384
MATCH = 4
LANES = 128
HIGH = 4
CAP = 2
SUB = 8
UNROLL = 13
F32 = jnp.float32
BF16 = jnp.bfloat16


def iota(shape, dim):
    return lax.broadcasted_iota(jnp.int32, shape, dim)


def take_lanes(values, index):
    return jnp.take_along_axis(values, index, axis=1, mode="promise_in_bounds")


def row_of(block, row, count=SUB):
    return jnp.broadcast_to(block[row : row + 1, :], (count, LANES))


def basis_of(s):
    remain = 1.0 - s
    square = s * s
    cube = square * s
    return (
        remain * remain * remain * (1.0 / 6.0),
        (3.0 * cube - 6.0 * square + 4.0) * (1.0 / 6.0),
        (-3.0 * cube + 3.0 * square + 3.0 * s + 1.0) * (1.0 / 6.0),
        cube * (1.0 / 6.0),
    )


def split_two(values):
    high = values.astype(BF16)
    low = (values - high.astype(F32)).astype(BF16)
    return jnp.concatenate([high, low], axis=1)


def places():
    return iota((LANES, LANES), 0).astype(F32).astype(BF16)


def spread(place, knot, kinds):
    low = jnp.bitwise_and(knot, LANES - 1).astype(F32)
    high = jnp.right_shift(knot, 7)
    low = jnp.concatenate([low, low], axis=0).astype(BF16)
    low = jnp.concatenate([low] * (LANES // 16), axis=0)
    hot = jnp.where(place == low, jnp.ones((), BF16), jnp.zeros((), BF16))
    hot = jnp.concatenate([hot, hot], axis=1)
    masks = []
    for h in range(HIGH):
        mask = jnp.where(high == h, 1.0, 0.0)
        mask = jnp.concatenate([mask, mask], axis=0).astype(BF16)
        mask = jnp.concatenate([mask, mask], axis=0)
        masks.append(jnp.concatenate([mask, mask], axis=1))
    sums = []
    for kind in kinds:
        parts = split_two(jnp.concatenate(kind, axis=0))
        left = jnp.concatenate([parts * mask for mask in masks], axis=0)
        sums.append(
            lax.dot_general(left, hot, (((1,), (1,)), ((), ())), preferred_element_type=F32)
        )
    return jnp.concatenate(sums, axis=0)


def fold_shifts(acc, base):
    lane = iota((SUB, LANES), 1)
    out = []
    before = None
    for h in range(HIGH):
        tiles = [acc[base + h * 32 + k * SUB : base + h * 32 + (k + 1) * SUB, :] for k in range(4)]
        rolled = [None] + [pltpu.roll(tiles[k], k, axis=1) for k in range(1, 4)]
        total = tiles[0]
        for k in range(1, 4):
            other = before[k] if before is not None else jnp.zeros((SUB, LANES), F32)
            total = total + jnp.where(lane >= k, rolled[k], other)
        out.append(total)
        before = rolled
    return out


def shift_tiles(shifted, tiles_ref):
    lane = iota((SUB, LANES), 1)
    for a in range(tiles_ref.shape[0]):
        tiles = [tiles_ref[a, h] for h in range(HIGH)]
        for k in range(4):
            rolled = [pltpu.roll(t, LANES - k, axis=1) for t in tiles] if k else tiles
            for h in range(HIGH):
                after = rolled[min(h + 1, HIGH - 1)]
                shifted[a, k, h] = jnp.where(lane < LANES - k, rolled[h], after) if k else rolled[h]


def gather_value(shifted, drive, knot, basis, normals):
    low = jnp.bitwise_and(knot, LANES - 1)
    high = jnp.right_shift(knot, 7)
    here = [high == h for h in range(HIGH - 1)]
    total = None
    for k in range(4):
        value = take_lanes(shifted[drive, k, HIGH - 1], low)
        for h in range(HIGH - 1):
            value = jnp.where(here[h], take_lanes(shifted[drive, k, h], low), value)
        term = basis[k] * value
        total = term if total is None else total + term
    return jnp.sum(normals * total, axis=0, keepdims=True)


def own_tile(own_ref, h, a):
    normals = own_ref[h, a, 0:SUB, :]
    info = own_ref[h, a, SUB : 2 * SUB, :]
    return normals, row_of(info, 0).astype(jnp.int32), basis_of(row_of(info, 1)), row_of(info, 2)


def inc_tile(inc_ref, block, rank):
    tile = jnp.concatenate([inc_ref[block, 2 * rank], inc_ref[block, 2 * rank + 1]], axis=0)
    info = inc_ref[block, 4]
    knot = jnp.where(rank == 0, info[0:1], info[1:2])
    normals = jnp.where(iota((SUB, LANES), 0) < DOF, tile, 0.0)
    knot = jnp.broadcast_to(knot, (SUB, LANES)).astype(jnp.int32)
    return normals, knot, basis_of(row_of(tile, 6)), row_of(tile, 7)


def decode(code, street_size):
    pick = jnp.bitwise_and(code, 3)
    tile = jnp.right_shift(code, 2)
    rank = jnp.bitwise_and(tile, 1)
    block = jnp.right_shift(tile, 1)
    shift = street_size.bit_length() - 1
    assert street_size == 1 << shift
    lane = jnp.right_shift(block, shift)
    part = jnp.bitwise_and(block, street_size - 1)
    return pick, rank, block, lane, part


def send_kernel(
    counts, dev, picks, knot_own, knot_par, match, spline, geometry, weight, resid,
    send, own, tab,
):
    drives = counts.shape[0]
    street_size = send.shape[1]
    lane = lax.axis_index("drive")
    street = lax.axis_index("street")
    tab[2 * drives * MATCH] = street
    entries = drives * MATCH
    dests = [dev[e % MATCH, lane * drives + e // MATCH] for e in range(entries)]
    ranks = []
    for e in range(entries):
        rank = 0
        for other in range(e // MATCH * MATCH):
            rank = rank + jnp.where(dests[other] == dests[e], 1, 0)
        ranks.append(rank)
        tab[e] = dests[e]
        tab[entries + e] = rank
    for j in range(send.shape[0]):
        for t in range(street_size):
            send[j, t, 4] = jnp.zeros((4, LANES), F32)
    slot = street * LANES + iota((1, LANES), 1)
    zero1 = jnp.zeros((1, LANES), F32)
    for a in range(drives):
        w = jnp.where(slot < counts[a], weight[a : a + 1, :], 0.0)
        root = jnp.sqrt(w)
        rho = -(root * resid[a : a + 1, :])
        own[a, 0:SUB, :] = jnp.concatenate(
            [geometry[d, a : a + 1, :] * root for d in range(DOF)] + [zero1] * 2, axis=0
        )
        own[a, SUB : 2 * SUB, :] = jnp.concatenate(
            [knot_own[a : a + 1, :].astype(F32), spline[0, a : a + 1, :], rho] + [zero1] * 5, axis=0
        )
        tile = jnp.concatenate(
            [-(geometry[DOF + d, a : a + 1, :] * root) for d in range(DOF)]
            + [spline[1, a : a + 1, :], rho],
            axis=0,
        )
        knots = knot_par[a : a + 1, :].astype(F32)
        matches = jnp.broadcast_to(match[a : a + 1, :], (SUB, LANES))
        some_live = counts[a] > street * LANES
        for m in range(MATCH):
            e = a * MATCH + m
            flag = jnp.where(some_live, picks[m, lane * drives + a] + 1, 0).astype(F32)
            normals = jnp.where(matches == m, tile, 0.0)
            flags = jnp.full((1, LANES), flag, F32)
            for t in range(street_size):
                for half in range(2):
                    send[dests[e], t, 2 * ranks[e] + half] = normals[4 * half : 4 * half + 4]
                send[dests[e], t, 4, pl.ds(ranks[e], 1), :] = knots
                send[dests[e], t, 4, pl.ds(CAP + ranks[e], 1), :] = flags


def read_places(tab, street_size, entries):
    return [(tab[e], tab[entries + e] * street_size) for e in range(entries)]


def put_values(out_ref, tab, own_ref, inc_ref, lst, tiles_ref, shifted):
    street_size, drives = own_ref.shape[0], own_ref.shape[1]
    at = read_places(tab, street_size, drives * MATCH)
    shift_tiles(shifted, tiles_ref)
    for a in range(drives):
        for s in range(street_size):
            normals, knot, basis, _ = own_tile(own_ref, s, a)
            value = gather_value(shifted, a, knot, basis, normals)
            for m in range(MATCH):
                lane, first = at[a * MATCH + m]
                out_ref[lane, first + s] = value

    def one(code):
        pick, rank, block, lane, part = decode(code, street_size)
        normals, knot, basis, _ = inc_tile(inc_ref, block, rank)
        value = gather_value(shifted, pick, knot, basis, normals)
        out_ref[lane, (CAP + rank) * street_size + part] = value

    count = lst[lst.shape[0] - 1]

    def some(i, carry):
        for j in range(UNROLL):
            one(lst[UNROLL * i + j])
        return carry

    lax.fori_loop(0, lax.div(count + UNROLL - 1, UNROLL), some, 0)


def own_sum(sent, got, at, a, s, street_size):
    lane, first = at[a * MATCH]
    total = sent[lane, first + s]
    for lane, first in at[a * MATCH : (a + 1) * MATCH]:
        total = total + got[lane, first + CAP * street_size + s]
    return total


def inc_sum(sent, got, rank, lane, part, street_size):
    return (
        got[lane, rank * street_size + part]
        + sent[lane, (CAP + rank) * street_size + part]
    )


def spread_own(acc, own_ref, kinds_own):
    street_size, drives = own_ref.shape[0], own_ref.shape[1]
    place = places()
    for a in range(drives):
        total = None
        for s in range(street_size):
            normals, knot, basis, rho = own_tile(own_ref, s, a)
            coeffs = [basis[k] * normals for k in range(4)]
            part = spread(place, knot, kinds_own(coeffs, rho, a, s))
            total = part if total is None else total + part
        acc[a] = total


def spread_inc(acc, street_size, inc_ref, lst, kinds_inc):
    place = places()
    count = lst[lst.shape[0] - 1]

    def one(index):
        pick, rank, block, lane, part = decode(lst[index], street_size)
        normals, knot, basis, rho = inc_tile(inc_ref, block, rank)
        normals = jnp.where(index < count, normals, 0.0)
        coeffs = [basis[k] * normals for k in range(4)]
        return pick, spread(place, knot, kinds_inc(coeffs, rho, rank, lane, part))

    def some(i, carry):
        for pick, value in [one(UNROLL * i + j) for j in range(UNROLL)]:
            acc[pick] = acc[pick] + value
        return carry

    lax.fori_loop(0, lax.div(count + UNROLL - 1, UNROLL), some, 0)


def start_kinds(coeffs, rho, *_):
    return [[c * rho for c in coeffs], [c * c for c in coeffs]]


def own_kernel(own, acc):
    spread_own(acc, own, start_kinds)


def start_kernel(tab, own, inc, begun, grad, diag, direction, out, lst, acc, shifted):
    drives = own.shape[1]
    street_size = own.shape[0]
    blocks = inc.shape[0]
    count = 0
    for first in range(0, blocks, 4):
        digits = inc[first, 4]
        for i in range(1, 4):
            digits = digits + inc[first + i, 4] * float(8**i)
        digits = (digits[2:3] + digits[3:4] * float(8**4)).astype(jnp.int32)[0, 0]
        for i in range(4):
            for r in range(CAP):
                flag = jnp.bitwise_and(jnp.right_shift(digits, 3 * (4 * r + i)), 7)
                lst[count] = ((first + i) * CAP + r) * 4 + flag - 1
                count = count + jnp.where(flag > 0, 1, 0)
    last = lst[jnp.maximum(count - 1, 0)]
    for i in range(UNROLL - 1):
        lst[count + i] = last
    lst[lst.shape[0] - 1] = count

    acc[...] = begun[...]
    spread_inc(acc, street_size, inc, lst, start_kinds)
    for a in range(drives):
        sums = acc[a]
        gradient = fold_shifts(sums, 0)
        squares = fold_shifts(sums, 128)
        for h in range(HIGH):
            diagonal = 1.0 + squares[h]
            grad[a, h] = gradient[h]
            diag[a, h] = diagonal
            direction[a, h] = gradient[h] / diagonal
    out[...] = jnp.zeros(out.shape, F32)
    put_values(out, tab, own, inc, lst, direction, shifted)


def scalar_row(values):
    lane = iota((1, LANES), 1)
    row = jnp.zeros((1, LANES), F32)
    for i, value in enumerate(values):
        total = jnp.sum(jnp.sum(value, axis=0, keepdims=True), axis=1, keepdims=True)
        row = jnp.where(lane == i, total, row)
    return row


def pick_lane(row, i):
    return jnp.sum(jnp.where(iota((1, LANES), 1) == i, row, 0.0), axis=1, keepdims=True)


def middle_kernel(
    tab, lst, own, inc, grad, diag, direction, sent, got, image, values, out, acc, ratio, shifted
):
    street_size, drives = own.shape[0], own.shape[1]
    at = read_places(tab, street_size, drives * MATCH)
    for a in range(drives):
        for s in range(street_size):
            values[pl.ds(s * drives + a, 1), :] = own_sum(sent, got, at, a, s, street_size)

    def kinds_own(coeffs, rho, a, s):
        value = jnp.broadcast_to(values[pl.ds(s * drives + a, 1), :], (SUB, LANES))
        return [[c * value for c in coeffs]]

    def kinds_inc(coeffs, rho, rank, lane, part):
        value = inc_sum(sent, got, rank, lane, part, street_size)
        value = jnp.broadcast_to(value, (SUB, LANES))
        return [[c * value for c in coeffs]]

    spread_own(acc, own, kinds_own)
    spread_inc(acc, street_size, inc, lst, kinds_inc)
    first = jnp.zeros((SUB, LANES), F32)
    second = jnp.zeros((SUB, LANES), F32)
    for a in range(drives):
        sums = fold_shifts(acc[a], 0)
        for h in range(HIGH):
            p = direction[a, h]
            q = p + sums[h]
            image[a, h] = q
            ratio[a, h] = q / diag[a, h]
            first = first + grad[a, h] * p
            second = second + p * q
    out[...] = jnp.zeros(out.shape, F32)
    put_values(out, tab, own, inc, lst, ratio, shifted)
    row = scalar_row([first, second])
    rows = 2 * CAP * street_size
    for j in range(out.shape[0]):
        out[j, rows] = row


def dots_kernel(tab, grad, diag, direction, image, values, sent, got, resid, precond, steps, out):
    drives = grad.shape[0]
    street_size = values.shape[0] // drives
    at = read_places(tab, street_size, drives * MATCH)
    rows = 2 * CAP * street_size
    total = got[0, rows]
    for j in range(1, got.shape[0]):
        total = total + got[j, rows]
    inner = pick_lane(total, 0)
    curve = pick_lane(total, 1)
    alpha = inner / curve
    one = jnp.zeros((SUB, LANES), F32)
    two = jnp.zeros((SUB, LANES), F32)
    three = jnp.zeros((SUB, LANES), F32)
    for a in range(drives):
        for h in range(HIGH):
            r = grad[a, h] - alpha * image[a, h]
            z = r / diag[a, h]
            resid[a, h] = r
            precond[a, h] = z
            one = one + r * z
            two = two + z * z
            three = three + z * direction[a, h]
    slots2 = jnp.zeros((1, LANES), F32)
    slots3 = jnp.zeros((1, LANES), F32)
    for a in range(drives):
        for s in range(street_size):
            before = values[pl.ds(s * drives + a, 1), :]
            value = before - alpha * own_sum(sent, got, at, a, s, street_size)
            slots2 = slots2 + value * value
            slots3 = slots3 + value * before
    head = iota((SUB, LANES), 0) == 0
    two = two + jnp.where(head, jnp.broadcast_to(slots2, (SUB, LANES)), 0.0)
    three = three + jnp.where(head, jnp.broadcast_to(slots3, (SUB, LANES)), 0.0)
    row = scalar_row([one, two, three])
    for j in range(out.shape[0]):
        out[j] = row
    lane = iota((SUB, LANES), 1)
    steps[...] = jnp.where(lane == 0, alpha, jnp.where(lane == 1, inner, curve))


def last_kernel(
    tab, lst, own, inc, direction, image, values, sent, got, sent2, got2, resid, precond,
    steps, o_p, o_z, o_r, o_h, o_q, acc, hess,
):
    street_size, drives = own.shape[0], own.shape[1]
    entries = drives * MATCH
    at = read_places(tab, street_size, entries)
    alpha = steps[0:1, 0:1]

    def kinds_own(coeffs, rho, a, s):
        value = values[pl.ds(s * drives + a, 1), :] - alpha * own_sum(
            sent2, got2, at, a, s, street_size
        )
        value = jnp.broadcast_to(value, (SUB, LANES))
        return [[c * value for c in coeffs]]

    def kinds_inc(coeffs, rho, rank, lane, part):
        value = inc_sum(sent, got, rank, lane, part, street_size) - alpha * inc_sum(
            sent2, got2, rank, lane, part, street_size
        )
        value = jnp.broadcast_to(value, (SUB, LANES))
        return [[c * value for c in coeffs]]

    spread_own(acc, own, kinds_own)
    spread_inc(acc, street_size, inc, lst, kinds_inc)
    for a in range(drives):
        sums = fold_shifts(acc[a], 0)
        for h in range(HIGH):
            hess[a, h] = precond[a, h] + sums[h]
    blocks = o_p.shape[1]
    tiles = PARAMS // LANES
    row = iota((SUB, LANES), 0)
    points = []
    masks = []
    for q in range(tiles):
        entry = q * LANES + iota((SUB, LANES), 1)
        point = jnp.right_shift(entry * 10923, 16)
        points.append(point)
        masks.append(row == entry - point * DOF)
    for bl in range(blocks):
        block = tab[2 * entries] * blocks + bl
        high = jnp.right_shift(block, 1)
        offset = jnp.bitwise_and(block, 1) * (LANES // 2)
        indices = [offset + points[q] for q in range(tiles)]
        for a in range(drives):
            for source, target in (
                (direction, o_p), (precond, o_z), (resid, o_r), (hess, o_h), (image, o_q)
            ):
                tile = source[a, high]
                for q in range(tiles):
                    value = jnp.where(masks[q], take_lanes(tile, indices[q]), 0.0)
                    target[a, bl : bl + 1, q * LANES : (q + 1) * LANES] = jnp.sum(
                        value, axis=0, keepdims=True
                    )


def finish_kernel(steps, got, o_p, o_z, o_r, o_h, o_q, step_out, resid_out):
    total = got[0]
    for j in range(1, got.shape[0]):
        total = total + got[j]
    inner_next = pick_lane(total, 0)
    alpha = steps[0:1, 0:1]
    inner = steps[0:1, 1:2]
    curve = steps[0:1, 2:3]
    beta = inner_next / inner
    denominator = pick_lane(total, 1) + 2.0 * beta * pick_lane(total, 2) + beta * beta * curve
    last = inner_next / denominator
    for a in range(o_p.shape[0]):
        p = o_p[a]
        step_out[a] = alpha * p + last * (o_z[a] + beta * p)
        resid_out[a] = o_r[a] - last * (o_h[a] + beta * o_q[a])


def call(kernel, shapes, spaces_in, spaces_out, scratch=(), limit=40, **kwargs):
    where = {"s": pltpu.SMEM, "v": pltpu.VMEM}
    return pl.pallas_call(
        kernel,
        out_shape=[jax.ShapeDtypeStruct(s, d) for s, d in shapes],
        in_specs=[pl.BlockSpec(memory_space=where[c]) for c in spaces_in],
        out_specs=[pl.BlockSpec(memory_space=where[c]) for c in spaces_out],
        scratch_shapes=list(scratch),
        compiler_params=pltpu.CompilerParams(vmem_limit_bytes=limit * 1024 * 1024),
        **kwargs,
    )


def body(
    pt_count,
    partner_dev,
    partner_pick,
    knot_own,
    knot_partner,
    match_slot,
    spline,
    geometry,
    point_weight,
    point_resid,
):
    drives = knot_own.shape[0]
    lanes = lax.axis_size("drive")
    street_size = lax.axis_size("street")
    entries = drives * MATCH
    blocks = lanes * street_size
    param = ((drives, HIGH, SUB, LANES), F32)
    arrays = (
        pt_count, partner_dev.T, partner_pick.T, knot_own, knot_partner, match_slot,
        spline, geometry, point_weight, point_resid,
    )
    send, mine, tab = call(
        send_kernel,
        [
            ((lanes, street_size, 5, 4, LANES), F32),
            ((drives, 2 * SUB, LANES), F32),
            ((2 * entries + 1,), jnp.int32),
        ],
        "sssvvvvvvv",
        "vvs",
        name="send",
        limit=60,
    )(*arrays)
    if street_size == 2:
        peer = lax.ppermute(mine, "street", [(0, 1), (1, 0)])
        first = lax.axis_index("street") == 0
        own = jnp.stack([jnp.where(first, mine, peer), jnp.where(first, peer, mine)])
    else:
        own = lax.all_gather(mine, "street", axis=0, tiled=False)
    inc = lax.all_to_all(
        send.reshape(blocks, 5, 4, LANES), ("drive", "street"), split_axis=0, concat_axis=0, tiled=True
    )
    exchange = ((lanes, 2 * CAP * street_size, 1, LANES), F32)
    exchange2 = ((lanes, 2 * CAP * street_size + 1, 1, LANES), F32)
    acc = pltpu.VMEM((drives, 128, LANES), F32)
    shifted = pltpu.VMEM((drives, 4, HIGH, SUB, LANES), F32)
    list_size = CAP * blocks + UNROLL
    (begun,) = call(
        own_kernel,
        [((drives, 256, LANES), F32)],
        "v",
        "v",
        name="own",
        cost_estimate=pl.CostEstimate(flops=70000000, bytes_accessed=1000000, transcendentals=0),
    )(own)
    grad, diag, direction, sent, lst = call(
        start_kernel,
        [param, param, param, exchange, ((list_size,), jnp.int32)],
        "svvv",
        "vvvvs",
        [pltpu.VMEM((drives, 256, LANES), F32), shifted],
        name="start",
    )(tab, own, inc, begun)
    got = lax.all_to_all(sent, "drive", split_axis=0, concat_axis=0, tiled=True)
    image, values, sent2 = call(
        middle_kernel,
        [param, ((street_size * drives, LANES), F32), exchange2],
        "ssvvvvvvv",
        "vvv",
        [acc, pltpu.VMEM(param[0], F32), shifted],
        name="middle",
    )(tab, lst, own, inc, grad, diag, direction, sent, got)
    got2 = lax.all_to_all(sent2, "drive", split_axis=0, concat_axis=0, tiled=True)
    resid, precond, steps, sent3 = call(
        dots_kernel,
        [param, param, ((SUB, LANES), F32), ((lanes, 1, LANES), F32)],
        "svvvvvvv",
        "vvvv",
        name="dots",
    )(tab, grad, diag, direction, image, values, sent2, got2)
    got3 = lax.all_to_all(sent3, "drive", split_axis=0, concat_axis=0, tiled=True)
    shape = ((drives, NBLK // street_size, PARAMS), F32)
    parts = call(
        last_kernel,
        [shape] * 5,
        "ssvvvvvvvvvvvv",
        "vvvvv",
        [acc, pltpu.VMEM(param[0], F32)],
        name="last",
        cost_estimate=pl.CostEstimate(flops=200000000, bytes_accessed=8000000, transcendentals=0),
    )(tab, lst, own, inc, direction, image, values, sent, got, sent2, got2, resid, precond, steps)
    return tuple(
        call(finish_kernel, [shape, shape], "vvvvvvv", "vv", name="finish")(steps, got3, *parts)
    )


def solution(mesh):
    placed = (
        P(("region", "drive")),
        P("region", None),
        P("region", None),
        P(("region", "drive"), "street"),
        P(("region", "drive"), "street"),
        P(("region", "drive"), "street"),
        P(None, ("region", "drive"), "street"),
        P(None, ("region", "drive"), "street"),
        P(("region", "drive"), "street"),
        P(("region", "drive"), "street"),
    )
    return jax.shard_map(
        body,
        mesh=mesh,
        in_specs=placed,
        out_specs=(P(("region", "drive"), "street", None), P(("region", "drive"), "street", None)),
        check_vma=False,
    )
```

```python
import jax
import jax.numpy as jnp
from jax import lax
from jax.experimental import pallas as pl
from jax.experimental.pallas import tpu as pltpu
from jax.sharding import PartitionSpec as P

NBLK = 8
DOF = 6
PARAMS = 384
MATCH = 4
LANES = 128
HIGH = 4
CAP = 2
SUB = 8
UNROLL = 13
F32 = jnp.float32
BF16 = jnp.bfloat16


def iota(shape, dim):
    return lax.broadcasted_iota(jnp.int32, shape, dim)


def take_lanes(values, index):
    return jnp.take_along_axis(values, index, axis=1, mode="promise_in_bounds")


def row_of(block, row, count=SUB):
    return jnp.broadcast_to(block[row : row + 1, :], (count, LANES))


def basis_of(s):
    remain = 1.0 - s
    square = s * s
    cube = square * s
    return (
        remain * remain * remain * (1.0 / 6.0),
        (3.0 * cube - 6.0 * square + 4.0) * (1.0 / 6.0),
        (-3.0 * cube + 3.0 * square + 3.0 * s + 1.0) * (1.0 / 6.0),
        cube * (1.0 / 6.0),
    )


def split_two(values):
    high = values.astype(BF16)
    low = (values - high.astype(F32)).astype(BF16)
    return jnp.concatenate([high, low], axis=1)


def places():
    return iota((LANES, LANES), 0).astype(F32).astype(BF16)


def spread(place, knot, kinds):
    low = jnp.bitwise_and(knot, LANES - 1).astype(F32)
    high = jnp.right_shift(knot, 7)
    low = jnp.concatenate([low, low], axis=0).astype(BF16)
    low = jnp.concatenate([low] * (LANES // 16), axis=0)
    hot = jnp.where(place == low, jnp.ones((), BF16), jnp.zeros((), BF16))
    hot = jnp.concatenate([hot, hot], axis=1)
    masks = []
    for h in range(HIGH):
        mask = jnp.where(high == h, 1.0, 0.0)
        mask = jnp.concatenate([mask, mask], axis=0).astype(BF16)
        mask = jnp.concatenate([mask, mask], axis=0)
        masks.append(jnp.concatenate([mask, mask], axis=1))
    sums = []
    for kind in kinds:
        parts = split_two(jnp.concatenate(kind, axis=0))
        left = jnp.concatenate([parts * mask for mask in masks], axis=0)
        sums.append(
            lax.dot_general(left, hot, (((1,), (1,)), ((), ())), preferred_element_type=F32)
        )
    return jnp.concatenate(sums, axis=0)


def fold_shifts(acc, base):
    lane = iota((SUB, LANES), 1)
    out = []
    before = None
    for h in range(HIGH):
        tiles = [acc[base + h * 32 + k * SUB : base + h * 32 + (k + 1) * SUB, :] for k in range(4)]
        rolled = [None] + [pltpu.roll(tiles[k], k, axis=1) for k in range(1, 4)]
        total = tiles[0]
        for k in range(1, 4):
            other = before[k] if before is not None else jnp.zeros((SUB, LANES), F32)
            total = total + jnp.where(lane >= k, rolled[k], other)
        out.append(total)
        before = rolled
    return out


def shift_tiles(shifted, tiles_ref):
    lane = iota((SUB, LANES), 1)
    for a in range(tiles_ref.shape[0]):
        tiles = [tiles_ref[a, h] for h in range(HIGH)]
        for k in range(4):
            rolled = [pltpu.roll(t, LANES - k, axis=1) for t in tiles] if k else tiles
            for h in range(HIGH):
                after = rolled[min(h + 1, HIGH - 1)]
                shifted[a, k, h] = jnp.where(lane < LANES - k, rolled[h], after) if k else rolled[h]


def gather_value(shifted, drive, knot, basis, normals):
    low = jnp.bitwise_and(knot, LANES - 1)
    high = jnp.right_shift(knot, 7)
    here = [high == h for h in range(HIGH - 1)]
    total = None
    for k in range(4):
        value = take_lanes(shifted[drive, k, HIGH - 1], low)
        for h in range(HIGH - 1):
            value = jnp.where(here[h], take_lanes(shifted[drive, k, h], low), value)
        term = basis[k] * value
        total = term if total is None else total + term
    return jnp.sum(normals * total, axis=0, keepdims=True)


def own_tile(own_ref, h, a):
    normals = own_ref[h, a, 0:SUB, :]
    info = own_ref[h, a, SUB : 2 * SUB, :]
    return normals, row_of(info, 0).astype(jnp.int32), basis_of(row_of(info, 1)), row_of(info, 2)


def inc_tile(inc_ref, block, rank):
    tile = jnp.concatenate([inc_ref[block, 2 * rank], inc_ref[block, 2 * rank + 1]], axis=0)
    info = inc_ref[block, 4]
    knot = jnp.where(rank == 0, info[0:1], info[1:2])
    normals = jnp.where(iota((SUB, LANES), 0) < DOF, tile, 0.0)
    knot = jnp.broadcast_to(knot, (SUB, LANES)).astype(jnp.int32)
    return normals, knot, basis_of(row_of(tile, 6)), row_of(tile, 7)


def decode(code, street_size):
    pick = jnp.bitwise_and(code, 3)
    tile = jnp.right_shift(code, 2)
    rank = jnp.bitwise_and(tile, 1)
    block = jnp.right_shift(tile, 1)
    shift = street_size.bit_length() - 1
    assert street_size == 1 << shift
    lane = jnp.right_shift(block, shift)
    part = jnp.bitwise_and(block, street_size - 1)
    return pick, rank, block, lane, part


def send_kernel(
    counts, dev, picks, knot_own, knot_par, match, spline, geometry, weight, resid,
    send, own, tab,
):
    drives = counts.shape[0]
    street_size = send.shape[1]
    lane = lax.axis_index("drive")
    street = lax.axis_index("street")
    tab[2 * drives * MATCH] = street
    entries = drives * MATCH
    dests = [dev[e % MATCH, lane * drives + e // MATCH] for e in range(entries)]
    ranks = []
    for e in range(entries):
        rank = 0
        for other in range(e // MATCH * MATCH):
            rank = rank + jnp.where(dests[other] == dests[e], 1, 0)
        ranks.append(rank)
        tab[e] = dests[e]
        tab[entries + e] = rank
    for j in range(send.shape[0]):
        for t in range(street_size):
            send[j, t, 4] = jnp.zeros((4, LANES), F32)
    slot = street * LANES + iota((1, LANES), 1)
    zero1 = jnp.zeros((1, LANES), F32)
    for a in range(drives):
        w = jnp.where(slot < counts[a], weight[a : a + 1, :], 0.0)
        root = jnp.sqrt(w)
        rho = -(root * resid[a : a + 1, :])
        own[a, 0:SUB, :] = jnp.concatenate(
            [geometry[d, a : a + 1, :] * root for d in range(DOF)] + [zero1] * 2, axis=0
        )
        own[a, SUB : 2 * SUB, :] = jnp.concatenate(
            [knot_own[a : a + 1, :].astype(F32), spline[0, a : a + 1, :], rho] + [zero1] * 5, axis=0
        )
        tile = jnp.concatenate(
            [-(geometry[DOF + d, a : a + 1, :] * root) for d in range(DOF)]
            + [spline[1, a : a + 1, :], rho],
            axis=0,
        )
        knots = knot_par[a : a + 1, :].astype(F32)
        matches = jnp.broadcast_to(match[a : a + 1, :], (SUB, LANES))
        some_live = counts[a] > street * LANES
        for m in range(MATCH):
            e = a * MATCH + m
            flag = jnp.where(some_live, picks[m, lane * drives + a] + 1, 0).astype(F32)
            normals = jnp.where(matches == m, tile, 0.0)
            flags = jnp.full((1, LANES), flag, F32)
            for t in range(street_size):
                for half in range(2):
                    send[dests[e], t, 2 * ranks[e] + half] = normals[4 * half : 4 * half + 4]
                send[dests[e], t, 4, pl.ds(ranks[e], 1), :] = knots
                send[dests[e], t, 4, pl.ds(CAP + ranks[e], 1), :] = flags


def read_places(tab, street_size, entries):
    return [(tab[e], tab[entries + e] * street_size) for e in range(entries)]


def put_values(out_ref, tab, own_ref, inc_ref, lst, tiles_ref, shifted):
    street_size, drives = own_ref.shape[0], own_ref.shape[1]
    at = read_places(tab, street_size, drives * MATCH)
    shift_tiles(shifted, tiles_ref)
    for a in range(drives):
        for s in range(street_size):
            normals, knot, basis, _ = own_tile(own_ref, s, a)
            value = gather_value(shifted, a, knot, basis, normals)
            for m in range(MATCH):
                lane, first = at[a * MATCH + m]
                out_ref[lane, first + s] = value

    def one(code):
        pick, rank, block, lane, part = decode(code, street_size)
        normals, knot, basis, _ = inc_tile(inc_ref, block, rank)
        value = gather_value(shifted, pick, knot, basis, normals)
        out_ref[lane, (CAP + rank) * street_size + part] = value

    count = lst[lst.shape[0] - 1]

    def some(i, carry):
        for j in range(UNROLL):
            one(lst[UNROLL * i + j])
        return carry

    lax.fori_loop(0, lax.div(count + UNROLL - 1, UNROLL), some, 0)


def own_sum(sent, got, at, a, s, street_size):
    lane, first = at[a * MATCH]
    total = sent[lane, first + s]
    for lane, first in at[a * MATCH : (a + 1) * MATCH]:
        total = total + got[lane, first + CAP * street_size + s]
    return total


def inc_sum(sent, got, rank, lane, part, street_size):
    return (
        got[lane, rank * street_size + part]
        + sent[lane, (CAP + rank) * street_size + part]
    )


def spread_own(acc, own_ref, kinds_own):
    street_size, drives = own_ref.shape[0], own_ref.shape[1]
    place = places()
    for a in range(drives):
        total = None
        for s in range(street_size):
            normals, knot, basis, rho = own_tile(own_ref, s, a)
            coeffs = [basis[k] * normals for k in range(4)]
            part = spread(place, knot, kinds_own(coeffs, rho, a, s))
            total = part if total is None else total + part
        acc[a] = total


def spread_inc(acc, street_size, inc_ref, lst, kinds_inc):
    place = places()
    count = lst[lst.shape[0] - 1]

    def one(index):
        pick, rank, block, lane, part = decode(lst[index], street_size)
        normals, knot, basis, rho = inc_tile(inc_ref, block, rank)
        normals = jnp.where(index < count, normals, 0.0)
        coeffs = [basis[k] * normals for k in range(4)]
        return pick, spread(place, knot, kinds_inc(coeffs, rho, rank, lane, part))

    def some(i, carry):
        for pick, value in [one(UNROLL * i + j) for j in range(UNROLL)]:
            acc[pick] = acc[pick] + value
        return carry

    lax.fori_loop(0, lax.div(count + UNROLL - 1, UNROLL), some, 0)


def start_kinds(coeffs, rho, *_):
    return [[c * rho for c in coeffs], [c * c for c in coeffs]]


def own_kernel(own, acc):
    spread_own(acc, own, start_kinds)


def start_kernel(tab, own, inc, begun, grad, diag, direction, out, lst, acc, shifted):
    drives = own.shape[1]
    street_size = own.shape[0]
    blocks = inc.shape[0]
    count = 0
    for first in range(0, blocks, 4):
        digits = inc[first, 4]
        for i in range(1, 4):
            digits = digits + inc[first + i, 4] * float(8**i)
        digits = (digits[2:3] + digits[3:4] * float(8**4)).astype(jnp.int32)[0, 0]
        for i in range(4):
            for r in range(CAP):
                flag = jnp.bitwise_and(jnp.right_shift(digits, 3 * (4 * r + i)), 7)
                lst[count] = ((first + i) * CAP + r) * 4 + flag - 1
                count = count + jnp.where(flag > 0, 1, 0)
    last = lst[jnp.maximum(count - 1, 0)]
    for i in range(UNROLL - 1):
        lst[count + i] = last
    lst[lst.shape[0] - 1] = count

    acc[...] = begun[...]
    spread_inc(acc, street_size, inc, lst, start_kinds)
    for a in range(drives):
        sums = acc[a]
        gradient = fold_shifts(sums, 0)
        squares = fold_shifts(sums, 128)
        for h in range(HIGH):
            diagonal = 1.0 + squares[h]
            grad[a, h] = gradient[h]
            diag[a, h] = diagonal
            direction[a, h] = gradient[h] / diagonal
    out[...] = jnp.zeros(out.shape, F32)
    put_values(out, tab, own, inc, lst, direction, shifted)


def sum_rows(rows):
    while len(rows) > 1:
        rows = [a + b for a, b in zip(rows[::2], rows[1::2])] + rows[len(rows) // 2 * 2 :]
    return jnp.sum(rows[0], axis=1, keepdims=True)


def middle_kernel(
    tab, lst, own, inc, grad, diag, direction, sent, got, image, values, out, acc, ratio, shifted
):
    street_size, drives = own.shape[0], own.shape[1]
    at = read_places(tab, street_size, drives * MATCH)
    for a in range(drives):
        for s in range(street_size):
            values[pl.ds(s * drives + a, 1), :] = own_sum(sent, got, at, a, s, street_size)

    def kinds_own(coeffs, rho, a, s):
        value = jnp.broadcast_to(values[pl.ds(s * drives + a, 1), :], (SUB, LANES))
        return [[c * value for c in coeffs]]

    def kinds_inc(coeffs, rho, rank, lane, part):
        value = inc_sum(sent, got, rank, lane, part, street_size)
        value = jnp.broadcast_to(value, (SUB, LANES))
        return [[c * value for c in coeffs]]

    spread_own(acc, own, kinds_own)
    spread_inc(acc, street_size, inc, lst, kinds_inc)
    first = jnp.zeros((SUB, LANES), F32)
    second = jnp.zeros((SUB, LANES), F32)
    for a in range(drives):
        sums = fold_shifts(acc[a], 0)
        for h in range(HIGH):
            p = direction[a, h]
            q = p + sums[h]
            image[a, h] = q
            ratio[a, h] = q / diag[a, h]
            first = first + grad[a, h] * p
            second = second + p * q
    out[...] = jnp.zeros(out.shape, F32)
    put_values(out, tab, own, inc, lst, ratio, shifted)
    rows = 2 * CAP * street_size
    for i, value in enumerate((first, second)):
        row = jnp.sum(value, axis=0, keepdims=True)
        for j in range(out.shape[0]):
            out[j, rows + i] = row


def dots_kernel(tab, grad, diag, direction, image, values, sent, got, resid, precond, steps, out):
    drives = grad.shape[0]
    street_size = values.shape[0] // drives
    at = read_places(tab, street_size, drives * MATCH)
    rows = 2 * CAP * street_size
    inner = sum_rows([got[j, rows] for j in range(got.shape[0])])
    curve = sum_rows([got[j, rows + 1] for j in range(got.shape[0])])
    alpha = inner / curve
    one = jnp.zeros((SUB, LANES), F32)
    two = jnp.zeros((SUB, LANES), F32)
    three = jnp.zeros((SUB, LANES), F32)
    for a in range(drives):
        for h in range(HIGH):
            r = grad[a, h] - alpha * image[a, h]
            z = r / diag[a, h]
            resid[a, h] = r
            precond[a, h] = z
            one = one + r * z
            two = two + z * z
            three = three + z * direction[a, h]
    slots2 = jnp.zeros((1, LANES), F32)
    slots3 = jnp.zeros((1, LANES), F32)
    for a in range(drives):
        for s in range(street_size):
            before = values[pl.ds(s * drives + a, 1), :]
            value = before - alpha * own_sum(sent, got, at, a, s, street_size)
            slots2 = slots2 + value * value
            slots3 = slots3 + value * before
    head = iota((SUB, LANES), 0) == 0
    two = two + jnp.where(head, jnp.broadcast_to(slots2, (SUB, LANES)), 0.0)
    three = three + jnp.where(head, jnp.broadcast_to(slots3, (SUB, LANES)), 0.0)
    for i, value in enumerate((one, two, three)):
        row = jnp.sum(value, axis=0, keepdims=True)
        for j in range(out.shape[0]):
            out[j, i] = row
    lane = iota((SUB, LANES), 1)
    steps[...] = jnp.where(lane == 0, alpha, jnp.where(lane == 1, inner, curve))


def last_kernel(
    tab, lst, own, inc, direction, image, values, sent, got, sent2, got2, resid, precond,
    steps, o_p, o_z, o_r, o_h, o_q, acc, hess,
):
    street_size, drives = own.shape[0], own.shape[1]
    entries = drives * MATCH
    at = read_places(tab, street_size, entries)
    alpha = steps[0:1, 0:1]

    def kinds_own(coeffs, rho, a, s):
        value = values[pl.ds(s * drives + a, 1), :] - alpha * own_sum(
            sent2, got2, at, a, s, street_size
        )
        value = jnp.broadcast_to(value, (SUB, LANES))
        return [[c * value for c in coeffs]]

    def kinds_inc(coeffs, rho, rank, lane, part):
        value = inc_sum(sent, got, rank, lane, part, street_size) - alpha * inc_sum(
            sent2, got2, rank, lane, part, street_size
        )
        value = jnp.broadcast_to(value, (SUB, LANES))
        return [[c * value for c in coeffs]]

    spread_own(acc, own, kinds_own)
    spread_inc(acc, street_size, inc, lst, kinds_inc)
    for a in range(drives):
        sums = fold_shifts(acc[a], 0)
        for h in range(HIGH):
            hess[a, h] = precond[a, h] + sums[h]
    blocks = o_p.shape[1]
    tiles = PARAMS // LANES
    row = iota((SUB, LANES), 0)
    points = []
    masks = []
    for q in range(tiles):
        entry = q * LANES + iota((SUB, LANES), 1)
        point = jnp.right_shift(entry * 10923, 16)
        points.append(point)
        masks.append(row == entry - point * DOF)
    for bl in range(blocks):
        block = tab[2 * entries] * blocks + bl
        high = jnp.right_shift(block, 1)
        offset = jnp.bitwise_and(block, 1) * (LANES // 2)
        indices = [offset + points[q] for q in range(tiles)]
        for a in range(drives):
            for source, target in (
                (direction, o_p), (precond, o_z), (resid, o_r), (hess, o_h), (image, o_q)
            ):
                tile = source[a, high]
                for q in range(tiles):
                    value = jnp.where(masks[q], take_lanes(tile, indices[q]), 0.0)
                    target[a, bl : bl + 1, q * LANES : (q + 1) * LANES] = jnp.sum(
                        value, axis=0, keepdims=True
                    )


def finish_kernel(steps, got, o_p, o_z, o_r, o_h, o_q, step_out, resid_out):
    inner_next, second, third = (
        sum_rows([got[j, i] for j in range(got.shape[0])]) for i in range(3)
    )
    alpha = steps[0:1, 0:1]
    inner = steps[0:1, 1:2]
    curve = steps[0:1, 2:3]
    beta = inner_next / inner
    denominator = second + 2.0 * beta * third + beta * beta * curve
    last = inner_next / denominator
    for a in range(o_p.shape[0]):
        p = o_p[a]
        step_out[a] = alpha * p + last * (o_z[a] + beta * p)
        resid_out[a] = o_r[a] - last * (o_h[a] + beta * o_q[a])


def call(kernel, shapes, spaces_in, spaces_out, scratch=(), limit=40, **kwargs):
    where = {"s": pltpu.SMEM, "v": pltpu.VMEM}
    return pl.pallas_call(
        kernel,
        out_shape=[jax.ShapeDtypeStruct(s, d) for s, d in shapes],
        in_specs=[pl.BlockSpec(memory_space=where[c]) for c in spaces_in],
        out_specs=[pl.BlockSpec(memory_space=where[c]) for c in spaces_out],
        scratch_shapes=list(scratch),
        compiler_params=pltpu.CompilerParams(vmem_limit_bytes=limit * 1024 * 1024),
        **kwargs,
    )


def body(
    pt_count,
    partner_dev,
    partner_pick,
    knot_own,
    knot_partner,
    match_slot,
    spline,
    geometry,
    point_weight,
    point_resid,
):
    drives = knot_own.shape[0]
    lanes = lax.axis_size("drive")
    street_size = lax.axis_size("street")
    entries = drives * MATCH
    blocks = lanes * street_size
    param = ((drives, HIGH, SUB, LANES), F32)
    arrays = (
        pt_count, partner_dev.T, partner_pick.T, knot_own, knot_partner, match_slot,
        spline, geometry, point_weight, point_resid,
    )
    send, mine, tab = call(
        send_kernel,
        [
            ((lanes, street_size, 5, 4, LANES), F32),
            ((drives, 2 * SUB, LANES), F32),
            ((2 * entries + 1,), jnp.int32),
        ],
        "sssvvvvvvv",
        "vvs",
        name="send",
        limit=60,
    )(*arrays)
    if street_size == 2:
        peer = lax.ppermute(mine, "street", [(0, 1), (1, 0)])
        first = lax.axis_index("street") == 0
        own = jnp.stack([jnp.where(first, mine, peer), jnp.where(first, peer, mine)])
    else:
        own = lax.all_gather(mine, "street", axis=0, tiled=False)
    inc = lax.all_to_all(
        send.reshape(blocks, 5, 4, LANES), ("drive", "street"), split_axis=0, concat_axis=0, tiled=True
    )
    exchange = ((lanes, 2 * CAP * street_size, 1, LANES), F32)
    exchange2 = ((lanes, 2 * CAP * street_size + 2, 1, LANES), F32)
    acc = pltpu.VMEM((drives, 128, LANES), F32)
    shifted = pltpu.VMEM((drives, 4, HIGH, SUB, LANES), F32)
    list_size = CAP * blocks + UNROLL
    (begun,) = call(
        own_kernel,
        [((drives, 256, LANES), F32)],
        "v",
        "v",
        name="own",
        cost_estimate=pl.CostEstimate(flops=70000000, bytes_accessed=1000000, transcendentals=0),
    )(own)
    grad, diag, direction, sent, lst = call(
        start_kernel,
        [param, param, param, exchange, ((list_size,), jnp.int32)],
        "svvv",
        "vvvvs",
        [pltpu.VMEM((drives, 256, LANES), F32), shifted],
        name="start",
    )(tab, own, inc, begun)
    got = lax.all_to_all(sent, "drive", split_axis=0, concat_axis=0, tiled=True)
    image, values, sent2 = call(
        middle_kernel,
        [param, ((street_size * drives, LANES), F32), exchange2],
        "ssvvvvvvv",
        "vvv",
        [acc, pltpu.VMEM(param[0], F32), shifted],
        name="middle",
    )(tab, lst, own, inc, grad, diag, direction, sent, got)
    got2 = lax.all_to_all(sent2, "drive", split_axis=0, concat_axis=0, tiled=True)
    resid, precond, steps, sent3 = call(
        dots_kernel,
        [param, param, ((SUB, LANES), F32), ((lanes, 3, 1, LANES), F32)],
        "svvvvvvv",
        "vvvv",
        name="dots",
    )(tab, grad, diag, direction, image, values, sent2, got2)
    got3 = lax.all_to_all(sent3, "drive", split_axis=0, concat_axis=0, tiled=True)
    shape = ((drives, NBLK // street_size, PARAMS), F32)
    parts = call(
        last_kernel,
        [shape] * 5,
        "ssvvvvvvvvvvvv",
        "vvvvv",
        [acc, pltpu.VMEM(param[0], F32)],
        name="last",
        cost_estimate=pl.CostEstimate(flops=200000000, bytes_accessed=8000000, transcendentals=0),
    )(tab, lst, own, inc, direction, image, values, sent, got, sent2, got2, resid, precond, steps)
    return tuple(
        call(finish_kernel, [shape, shape], "vvvvvvv", "vv", name="finish")(steps, got3, *parts)
    )


def solution(mesh):
    placed = (
        P(("region", "drive")),
        P("region", None),
        P("region", None),
        P(("region", "drive"), "street"),
        P(("region", "drive"), "street"),
        P(("region", "drive"), "street"),
        P(None, ("region", "drive"), "street"),
        P(None, ("region", "drive"), "street"),
        P(("region", "drive"), "street"),
        P(("region", "drive"), "street"),
    )
    return jax.shard_map(
        body,
        mesh=mesh,
        in_specs=placed,
        out_specs=(P(("region", "drive"), "street", None), P(("region", "drive"), "street", None)),
        check_vma=False,
    )
```

```python
import jax
import jax.numpy as jnp
from jax import lax
from jax.experimental import pallas as pl
from jax.experimental.pallas import tpu as pltpu
from jax.sharding import PartitionSpec as P

NBLK = 8
DOF = 6
PARAMS = 384
MATCH = 4
LANES = 128
HIGH = 4
CAP = 2
SUB = 8
UNROLL = 14
F32 = jnp.float32
BF16 = jnp.bfloat16


def iota(shape, dim):
    return lax.broadcasted_iota(jnp.int32, shape, dim)


def take_lanes(values, index):
    return jnp.take_along_axis(values, index, axis=1, mode="promise_in_bounds")


def row_of(block, row, count=SUB):
    return jnp.broadcast_to(block[row : row + 1, :], (count, LANES))


def basis_of(s):
    remain = 1.0 - s
    square = s * s
    cube = square * s
    return (
        remain * remain * remain * (1.0 / 6.0),
        (3.0 * cube - 6.0 * square + 4.0) * (1.0 / 6.0),
        (-3.0 * cube + 3.0 * square + 3.0 * s + 1.0) * (1.0 / 6.0),
        cube * (1.0 / 6.0),
    )


def split_two(values):
    high = values.astype(BF16)
    low = (values - high.astype(F32)).astype(BF16)
    return jnp.concatenate([high, low], axis=1)


def places():
    return iota((LANES, LANES), 0).astype(F32).astype(BF16)


def spread(place, knot, kinds):
    low = jnp.bitwise_and(knot, LANES - 1).astype(F32)
    high = jnp.right_shift(knot, 7)
    low = jnp.concatenate([low, low], axis=0).astype(BF16)
    low = jnp.concatenate([low] * (LANES // 16), axis=0)
    hot = jnp.where(place == low, jnp.ones((), BF16), jnp.zeros((), BF16))
    hot = jnp.concatenate([hot, hot], axis=1)
    masks = []
    for h in range(HIGH):
        mask = jnp.where(high == h, 1.0, 0.0)
        mask = jnp.concatenate([mask, mask], axis=0).astype(BF16)
        mask = jnp.concatenate([mask, mask], axis=0)
        masks.append(jnp.concatenate([mask, mask], axis=1))
    sums = []
    for kind in kinds:
        parts = split_two(jnp.concatenate(kind, axis=0))
        left = jnp.concatenate([parts * mask for mask in masks], axis=0)
        sums.append(
            lax.dot_general(left, hot, (((1,), (1,)), ((), ())), preferred_element_type=F32)
        )
    return jnp.concatenate(sums, axis=0)


def fold_shifts(acc, base):
    lane = iota((SUB, LANES), 1)
    out = []
    before = None
    for h in range(HIGH):
        tiles = [acc[base + h * 32 + k * SUB : base + h * 32 + (k + 1) * SUB, :] for k in range(4)]
        rolled = [None] + [pltpu.roll(tiles[k], k, axis=1) for k in range(1, 4)]
        total = tiles[0]
        for k in range(1, 4):
            other = before[k] if before is not None else jnp.zeros((SUB, LANES), F32)
            total = total + jnp.where(lane >= k, rolled[k], other)
        out.append(total)
        before = rolled
    return out


def shift_tiles(shifted, tiles_ref):
    lane = iota((SUB, LANES), 1)
    for a in range(tiles_ref.shape[0]):
        tiles = [tiles_ref[a, h] for h in range(HIGH)]
        for k in range(4):
            rolled = [pltpu.roll(t, LANES - k, axis=1) for t in tiles] if k else tiles
            for h in range(HIGH):
                after = rolled[min(h + 1, HIGH - 1)]
                shifted[a, k, h] = jnp.where(lane < LANES - k, rolled[h], after) if k else rolled[h]


def gather_value(shifted, drive, knot, basis, normals):
    low = jnp.bitwise_and(knot, LANES - 1)
    high = jnp.right_shift(knot, 7)
    here = [high == h for h in range(HIGH - 1)]
    total = None
    for k in range(4):
        value = take_lanes(shifted[drive, k, HIGH - 1], low)
        for h in range(HIGH - 1):
            value = jnp.where(here[h], take_lanes(shifted[drive, k, h], low), value)
        term = basis[k] * value
        total = term if total is None else total + term
    return jnp.sum(normals * total, axis=0, keepdims=True)


def own_tile(own_ref, h, a):
    normals = own_ref[h, a, 0:SUB, :]
    info = own_ref[h, a, SUB : 2 * SUB, :]
    return normals, row_of(info, 0).astype(jnp.int32), basis_of(row_of(info, 1)), row_of(info, 2)


def inc_tile(inc_ref, block, rank):
    tile = jnp.concatenate([inc_ref[block, 2 * rank], inc_ref[block, 2 * rank + 1]], axis=0)
    info = inc_ref[block, 4]
    knot = jnp.where(rank == 0, info[0:1], info[1:2])
    normals = jnp.where(iota((SUB, LANES), 0) < DOF, tile, 0.0)
    knot = jnp.broadcast_to(knot, (SUB, LANES)).astype(jnp.int32)
    return normals, knot, basis_of(row_of(tile, 6)), row_of(tile, 7)


def decode(code, street_size):
    pick = jnp.bitwise_and(code, 3)
    tile = jnp.right_shift(code, 2)
    rank = jnp.bitwise_and(tile, 1)
    block = jnp.right_shift(tile, 1)
    shift = street_size.bit_length() - 1
    assert street_size == 1 << shift
    lane = jnp.right_shift(block, shift)
    part = jnp.bitwise_and(block, street_size - 1)
    return pick, rank, block, lane, part


def send_kernel(
    counts, dev, picks, knot_own, knot_par, match, spline, geometry, weight, resid,
    send, own, tab,
):
    drives = counts.shape[0]
    street_size = send.shape[1]
    lane = lax.axis_index("drive")
    street = lax.axis_index("street")
    tab[2 * drives * MATCH] = street
    entries = drives * MATCH
    dests = [dev[e % MATCH, lane * drives + e // MATCH] for e in range(entries)]
    ranks = []
    for e in range(entries):
        rank = 0
        for other in range(e // MATCH * MATCH):
            rank = rank + jnp.where(dests[other] == dests[e], 1, 0)
        ranks.append(rank)
        tab[e] = dests[e]
        tab[entries + e] = rank
    for j in range(send.shape[0]):
        for t in range(street_size):
            send[j, t, 4] = jnp.zeros((4, LANES), F32)
    slot = street * LANES + iota((1, LANES), 1)
    zero1 = jnp.zeros((1, LANES), F32)
    for a in range(drives):
        w = jnp.where(slot < counts[a], weight[a : a + 1, :], 0.0)
        root = jnp.sqrt(w)
        rho = -(root * resid[a : a + 1, :])
        own[a, 0:SUB, :] = jnp.concatenate(
            [geometry[d, a : a + 1, :] * root for d in range(DOF)] + [zero1] * 2, axis=0
        )
        own[a, SUB : 2 * SUB, :] = jnp.concatenate(
            [knot_own[a : a + 1, :].astype(F32), spline[0, a : a + 1, :], rho] + [zero1] * 5, axis=0
        )
        tile = jnp.concatenate(
            [-(geometry[DOF + d, a : a + 1, :] * root) for d in range(DOF)]
            + [spline[1, a : a + 1, :], rho],
            axis=0,
        )
        knots = knot_par[a : a + 1, :].astype(F32)
        matches = jnp.broadcast_to(match[a : a + 1, :], (SUB, LANES))
        some_live = counts[a] > street * LANES
        for m in range(MATCH):
            e = a * MATCH + m
            flag = jnp.where(some_live, picks[m, lane * drives + a] + 1, 0).astype(F32)
            normals = jnp.where(matches == m, tile, 0.0)
            flags = jnp.full((1, LANES), flag, F32)
            for t in range(street_size):
                for half in range(2):
                    send[dests[e], t, 2 * ranks[e] + half] = normals[4 * half : 4 * half + 4]
                send[dests[e], t, 4, pl.ds(ranks[e], 1), :] = knots
                send[dests[e], t, 4, pl.ds(CAP + ranks[e], 1), :] = flags


def read_places(tab, street_size, entries):
    return [(tab[e], tab[entries + e] * street_size) for e in range(entries)]


def put_values(out_ref, tab, own_ref, inc_ref, lst, tiles_ref, shifted):
    street_size, drives = own_ref.shape[0], own_ref.shape[1]
    at = read_places(tab, street_size, drives * MATCH)
    shift_tiles(shifted, tiles_ref)
    for a in range(drives):
        for s in range(street_size):
            normals, knot, basis, _ = own_tile(own_ref, s, a)
            value = gather_value(shifted, a, knot, basis, normals)
            for m in range(MATCH):
                lane, first = at[a * MATCH + m]
                out_ref[lane, first + s] = value

    def one(code):
        pick, rank, block, lane, part = decode(code, street_size)
        normals, knot, basis, _ = inc_tile(inc_ref, block, rank)
        value = gather_value(shifted, pick, knot, basis, normals)
        out_ref[lane, (CAP + rank) * street_size + part] = value

    count = lst[lst.shape[0] - 1]

    def some(i, carry):
        for j in range(UNROLL):
            one(lst[UNROLL * i + j])
        return carry

    lax.fori_loop(0, lax.div(count + UNROLL - 1, UNROLL), some, 0)


def own_sum(sent, got, at, a, s, street_size):
    lane, first = at[a * MATCH]
    total = sent[lane, first + s]
    for lane, first in at[a * MATCH : (a + 1) * MATCH]:
        total = total + got[lane, first + CAP * street_size + s]
    return total


def inc_sum(sent, got, rank, lane, part, street_size):
    return (
        got[lane, rank * street_size + part]
        + sent[lane, (CAP + rank) * street_size + part]
    )


def spread_own(acc, own_ref, kinds_own):
    street_size, drives = own_ref.shape[0], own_ref.shape[1]
    place = places()
    for a in range(drives):
        total = None
        for s in range(street_size):
            normals, knot, basis, rho = own_tile(own_ref, s, a)
            coeffs = [basis[k] * normals for k in range(4)]
            part = spread(place, knot, kinds_own(coeffs, rho, a, s))
            total = part if total is None else total + part
        acc[a] = total


def spread_inc(acc, street_size, inc_ref, lst, kinds_inc):
    place = places()
    count = lst[lst.shape[0] - 1]

    def one(index):
        pick, rank, block, lane, part = decode(lst[index], street_size)
        normals, knot, basis, rho = inc_tile(inc_ref, block, rank)
        normals = jnp.where(index < count, normals, 0.0)
        coeffs = [basis[k] * normals for k in range(4)]
        return pick, spread(place, knot, kinds_inc(coeffs, rho, rank, lane, part))

    def some(i, carry):
        for pick, value in [one(UNROLL * i + j) for j in range(UNROLL)]:
            acc[pick] = acc[pick] + value
        return carry

    lax.fori_loop(0, lax.div(count + UNROLL - 1, UNROLL), some, 0)


def start_kinds(coeffs, rho, *_):
    return [[c * rho for c in coeffs], [c * c for c in coeffs]]


def own_kernel(own, acc):
    spread_own(acc, own, start_kinds)


def start_kernel(tab, own, inc, begun, grad, diag, direction, out, lst, acc, shifted):
    drives = own.shape[1]
    street_size = own.shape[0]
    blocks = inc.shape[0]
    count = 0
    for first in range(0, blocks, 4):
        digits = inc[first, 4]
        for i in range(1, 4):
            digits = digits + inc[first + i, 4] * float(8**i)
        digits = (digits[2:3] + digits[3:4] * float(8**4)).astype(jnp.int32)[0, 0]
        for i in range(4):
            for r in range(CAP):
                flag = jnp.bitwise_and(jnp.right_shift(digits, 3 * (4 * r + i)), 7)
                lst[count] = ((first + i) * CAP + r) * 4 + flag - 1
                count = count + jnp.where(flag > 0, 1, 0)
    last = lst[jnp.maximum(count - 1, 0)]
    for i in range(UNROLL - 1):
        lst[count + i] = last
    lst[lst.shape[0] - 1] = count

    acc[...] = begun[...]
    spread_inc(acc, street_size, inc, lst, start_kinds)
    for a in range(drives):
        sums = acc[a]
        gradient = fold_shifts(sums, 0)
        squares = fold_shifts(sums, 128)
        for h in range(HIGH):
            diagonal = 1.0 + squares[h]
            grad[a, h] = gradient[h]
            diag[a, h] = diagonal
            direction[a, h] = gradient[h] / diagonal
    out[...] = jnp.zeros(out.shape, F32)
    put_values(out, tab, own, inc, lst, direction, shifted)


def sum_rows(rows):
    while len(rows) > 1:
        rows = [a + b for a, b in zip(rows[::2], rows[1::2])] + rows[len(rows) // 2 * 2 :]
    return jnp.sum(rows[0], axis=1, keepdims=True)


def middle_kernel(
    tab, lst, own, inc, grad, diag, direction, sent, got, image, values, out, acc, ratio, shifted
):
    street_size, drives = own.shape[0], own.shape[1]
    at = read_places(tab, street_size, drives * MATCH)
    for a in range(drives):
        for s in range(street_size):
            values[pl.ds(s * drives + a, 1), :] = own_sum(sent, got, at, a, s, street_size)

    def kinds_own(coeffs, rho, a, s):
        value = jnp.broadcast_to(values[pl.ds(s * drives + a, 1), :], (SUB, LANES))
        return [[c * value for c in coeffs]]

    def kinds_inc(coeffs, rho, rank, lane, part):
        value = inc_sum(sent, got, rank, lane, part, street_size)
        value = jnp.broadcast_to(value, (SUB, LANES))
        return [[c * value for c in coeffs]]

    spread_own(acc, own, kinds_own)
    spread_inc(acc, street_size, inc, lst, kinds_inc)
    first = jnp.zeros((SUB, LANES), F32)
    second = jnp.zeros((SUB, LANES), F32)
    for a in range(drives):
        sums = fold_shifts(acc[a], 0)
        for h in range(HIGH):
            p = direction[a, h]
            q = p + sums[h]
            image[a, h] = q
            ratio[a, h] = q / diag[a, h]
            first = first + grad[a, h] * p
            second = second + p * q
    out[...] = jnp.zeros(out.shape, F32)
    put_values(out, tab, own, inc, lst, ratio, shifted)
    rows = 2 * CAP * street_size
    for i, value in enumerate((first, second)):
        row = jnp.sum(value, axis=0, keepdims=True)
        for j in range(out.shape[0]):
            out[j, rows + i] = row


def dots_kernel(tab, grad, diag, direction, image, values, sent, got, resid, precond, steps, out):
    drives = grad.shape[0]
    street_size = values.shape[0] // drives
    at = read_places(tab, street_size, drives * MATCH)
    rows = 2 * CAP * street_size
    inner = sum_rows([got[j, rows] for j in range(got.shape[0])])
    curve = sum_rows([got[j, rows + 1] for j in range(got.shape[0])])
    alpha = inner / curve
    one = jnp.zeros((SUB, LANES), F32)
    two = jnp.zeros((SUB, LANES), F32)
    three = jnp.zeros((SUB, LANES), F32)
    for a in range(drives):
        for h in range(HIGH):
            r = grad[a, h] - alpha * image[a, h]
            z = r / diag[a, h]
            resid[a, h] = r
            precond[a, h] = z
            one = one + r * z
            two = two + z * z
            three = three + z * direction[a, h]
    slots2 = jnp.zeros((1, LANES), F32)
    slots3 = jnp.zeros((1, LANES), F32)
    for a in range(drives):
        for s in range(street_size):
            before = values[pl.ds(s * drives + a, 1), :]
            value = before - alpha * own_sum(sent, got, at, a, s, street_size)
            slots2 = slots2 + value * value
            slots3 = slots3 + value * before
    head = iota((SUB, LANES), 0) == 0
    two = two + jnp.where(head, jnp.broadcast_to(slots2, (SUB, LANES)), 0.0)
    three = three + jnp.where(head, jnp.broadcast_to(slots3, (SUB, LANES)), 0.0)
    for i, value in enumerate((one, two, three)):
        row = jnp.sum(value, axis=0, keepdims=True)
        for j in range(out.shape[0]):
            out[j, i] = row
    lane = iota((SUB, LANES), 1)
    steps[...] = jnp.where(lane == 0, alpha, jnp.where(lane == 1, inner, curve))


def last_kernel(
    tab, lst, own, inc, direction, image, values, sent, got, sent2, got2, resid, precond,
    steps, o_p, o_z, o_r, o_h, o_q, acc, hess,
):
    street_size, drives = own.shape[0], own.shape[1]
    entries = drives * MATCH
    at = read_places(tab, street_size, entries)
    alpha = steps[0:1, 0:1]

    def kinds_own(coeffs, rho, a, s):
        value = values[pl.ds(s * drives + a, 1), :] - alpha * own_sum(
            sent2, got2, at, a, s, street_size
        )
        value = jnp.broadcast_to(value, (SUB, LANES))
        return [[c * value for c in coeffs]]

    def kinds_inc(coeffs, rho, rank, lane, part):
        value = inc_sum(sent, got, rank, lane, part, street_size) - alpha * inc_sum(
            sent2, got2, rank, lane, part, street_size
        )
        value = jnp.broadcast_to(value, (SUB, LANES))
        return [[c * value for c in coeffs]]

    spread_own(acc, own, kinds_own)
    spread_inc(acc, street_size, inc, lst, kinds_inc)
    for a in range(drives):
        sums = fold_shifts(acc[a], 0)
        for h in range(HIGH):
            hess[a, h] = precond[a, h] + sums[h]
    blocks = o_p.shape[1]
    tiles = PARAMS // LANES
    row = iota((SUB, LANES), 0)
    points = []
    masks = []
    for q in range(tiles):
        entry = q * LANES + iota((SUB, LANES), 1)
        point = jnp.right_shift(entry * 10923, 16)
        points.append(point)
        masks.append(row == entry - point * DOF)
    for bl in range(blocks):
        block = tab[2 * entries] * blocks + bl
        high = jnp.right_shift(block, 1)
        offset = jnp.bitwise_and(block, 1) * (LANES // 2)
        indices = [offset + points[q] for q in range(tiles)]
        for a in range(drives):
            for source, target in (
                (direction, o_p), (precond, o_z), (resid, o_r), (hess, o_h), (image, o_q)
            ):
                tile = source[a, high]
                for q in range(tiles):
                    value = jnp.where(masks[q], take_lanes(tile, indices[q]), 0.0)
                    target[a, bl : bl + 1, q * LANES : (q + 1) * LANES] = jnp.sum(
                        value, axis=0, keepdims=True
                    )


def finish_kernel(steps, got, o_p, o_z, o_r, o_h, o_q, step_out, resid_out):
    inner_next, second, third = (
        sum_rows([got[j, i] for j in range(got.shape[0])]) for i in range(3)
    )
    alpha = steps[0:1, 0:1]
    inner = steps[0:1, 1:2]
    curve = steps[0:1, 2:3]
    beta = inner_next / inner
    denominator = second + 2.0 * beta * third + beta * beta * curve
    last = inner_next / denominator
    for a in range(o_p.shape[0]):
        p = o_p[a]
        step_out[a] = alpha * p + last * (o_z[a] + beta * p)
        resid_out[a] = o_r[a] - last * (o_h[a] + beta * o_q[a])


def call(kernel, shapes, spaces_in, spaces_out, scratch=(), limit=40, **kwargs):
    where = {"s": pltpu.SMEM, "v": pltpu.VMEM}
    return pl.pallas_call(
        kernel,
        out_shape=[jax.ShapeDtypeStruct(s, d) for s, d in shapes],
        in_specs=[pl.BlockSpec(memory_space=where[c]) for c in spaces_in],
        out_specs=[pl.BlockSpec(memory_space=where[c]) for c in spaces_out],
        scratch_shapes=list(scratch),
        compiler_params=pltpu.CompilerParams(vmem_limit_bytes=limit * 1024 * 1024),
        **kwargs,
    )


def body(
    pt_count,
    partner_dev,
    partner_pick,
    knot_own,
    knot_partner,
    match_slot,
    spline,
    geometry,
    point_weight,
    point_resid,
):
    drives = knot_own.shape[0]
    lanes = lax.axis_size("drive")
    street_size = lax.axis_size("street")
    entries = drives * MATCH
    blocks = lanes * street_size
    param = ((drives, HIGH, SUB, LANES), F32)
    arrays = (
        pt_count, partner_dev.T, partner_pick.T, knot_own, knot_partner, match_slot,
        spline, geometry, point_weight, point_resid,
    )
    send, mine, tab = call(
        send_kernel,
        [
            ((lanes, street_size, 5, 4, LANES), F32),
            ((drives, 2 * SUB, LANES), F32),
            ((2 * entries + 1,), jnp.int32),
        ],
        "sssvvvvvvv",
        "vvs",
        name="send",
        limit=60,
    )(*arrays)
    if street_size == 2:
        peer = lax.ppermute(mine, "street", [(0, 1), (1, 0)])
        first = lax.axis_index("street") == 0
        own = jnp.stack([jnp.where(first, mine, peer), jnp.where(first, peer, mine)])
    else:
        own = lax.all_gather(mine, "street", axis=0, tiled=False)
    inc = lax.all_to_all(
        send.reshape(blocks, 5, 4, LANES), ("drive", "street"), split_axis=0, concat_axis=0, tiled=True
    )
    exchange = ((lanes, 2 * CAP * street_size, 1, LANES), F32)
    exchange2 = ((lanes, 2 * CAP * street_size + 2, 1, LANES), F32)
    acc = pltpu.VMEM((drives, 128, LANES), F32)
    shifted = pltpu.VMEM((drives, 4, HIGH, SUB, LANES), F32)
    list_size = CAP * blocks + UNROLL
    (begun,) = call(
        own_kernel,
        [((drives, 256, LANES), F32)],
        "v",
        "v",
        name="own",
        cost_estimate=pl.CostEstimate(flops=70000000, bytes_accessed=1000000, transcendentals=0),
    )(own)
    grad, diag, direction, sent, lst = call(
        start_kernel,
        [param, param, param, exchange, ((list_size,), jnp.int32)],
        "svvv",
        "vvvvs",
        [pltpu.VMEM((drives, 256, LANES), F32), shifted],
        name="start",
    )(tab, own, inc, begun)
    got = lax.all_to_all(sent, "drive", split_axis=0, concat_axis=0, tiled=True)
    image, values, sent2 = call(
        middle_kernel,
        [param, ((street_size * drives, LANES), F32), exchange2],
        "ssvvvvvvv",
        "vvv",
        [acc, pltpu.VMEM(param[0], F32), shifted],
        name="middle",
    )(tab, lst, own, inc, grad, diag, direction, sent, got)
    got2 = lax.all_to_all(sent2, "drive", split_axis=0, concat_axis=0, tiled=True)
    resid, precond, steps, sent3 = call(
        dots_kernel,
        [param, param, ((SUB, LANES), F32), ((lanes, 3, 1, LANES), F32)],
        "svvvvvvv",
        "vvvv",
        name="dots",
    )(tab, grad, diag, direction, image, values, sent2, got2)
    got3 = lax.all_to_all(sent3, "drive", split_axis=0, concat_axis=0, tiled=True)
    shape = ((drives, NBLK // street_size, PARAMS), F32)
    parts = call(
        last_kernel,
        [shape] * 5,
        "ssvvvvvvvvvvvv",
        "vvvvv",
        [acc, pltpu.VMEM(param[0], F32)],
        name="last",
        cost_estimate=pl.CostEstimate(flops=200000000, bytes_accessed=8000000, transcendentals=0),
    )(tab, lst, own, inc, direction, image, values, sent, got, sent2, got2, resid, precond, steps)
    return tuple(
        call(finish_kernel, [shape, shape], "vvvvvvv", "vv", name="finish")(steps, got3, *parts)
    )


def solution(mesh):
    placed = (
        P(("region", "drive")),
        P("region", None),
        P("region", None),
        P(("region", "drive"), "street"),
        P(("region", "drive"), "street"),
        P(("region", "drive"), "street"),
        P(None, ("region", "drive"), "street"),
        P(None, ("region", "drive"), "street"),
        P(("region", "drive"), "street"),
        P(("region", "drive"), "street"),
    )
    return jax.shard_map(
        body,
        mesh=mesh,
        in_specs=placed,
        out_specs=(P(("region", "drive"), "street", None), P(("region", "drive"), "street", None)),
        check_vma=False,
    )
```
